512 devices in a mesh: gx: 64 (over y, z), gy: 8 (over x, core).
Axes of the slice: x: 4, y: 8, z: 8, core: 2. Of those that a mesh axis runs over, the one named last changes fastest.
Arguments:
- features: float32 [32, 64, 256, 128], P(None, 'gx', 'gy'), may hold values from -6 to 6
- conv_weight: float32 [3, 3, 3, 32, 32], replicated, may hold values from -0.21875 to 0.21875
- conv_bias: float32 [32], replicated, may hold values from -3 to 3
- spectral_weight: float32 [4096, 2048], P(('gx', 'gy')), may hold values from -12 to 12
Outputs:
- layer_out: float32 [32, 64, 256, 128], P(None, 'gx', 'gy')
The draws below stay inside these ranges and needn't reach their ends.
All inputs are finite; a program needn't handle non-finite values.
Results may differ from the reference program's by a relative error of at most 0.000062.
Values sent between devices are 32-bit elements; how exact they have to be, the bound alone decides.
No kernel may reach another device: no remote copies, remote signals or barrier semaphores. Data moves between devices by JAX's collectives and lax.ppermute only.
A program may use at most 64 MiB of HBM per device.

```python
import math
import jax
import jax.numpy as jnp
from jax import lax

C = 32
KX = 16
KY = 16
KZ = 16
NZ = 128
NX = 64
NY = 256
PAIRS = 256
MODES = 4096


def block_scale(rng, dims, cuts, low, top_value):
    def one(position, shards_of):
        steps = jax.random.uniform(jax.random.fold_in(jax.random.fold_in(rng, 6), position), (shards_of,), jnp.float32, low / len(cuts), top_value / len(cuts))
        return jnp.repeat(jnp.exp(steps), dims[position] // shards_of).reshape((-1,) + (1,) * (len(dims) - position - 1))

    level = one(*cuts[0])
    for cut in cuts[1:]:
        level = level * one(*cut)
    return level


def centred(key, shape, scale, bound, cuts=(), kind=jnp.bfloat16):
    loudness = block_scale(key, shape, cuts, -0.22, 0.18) if cuts else 1.0
    drawn = jax.random.normal(key, shape, jnp.float32) * scale * loudness
    return jnp.minimum(jnp.maximum(drawn, -bound), bound).astype(kind)


def setup_inputs(seed: int = 0) -> dict:
    arg_keys = jax.random.split(jax.random.key(seed), 5)
    return {
        "features": centred(arg_keys[0], (C, NX, NY, NZ), 1.0, 6.0, ((1, 64), (2, 8)), jnp.float32),
        "conv_weight": centred(arg_keys[1], (3, 3, 3, C, C), (27 * C) ** -0.5, 0.21875, (), jnp.float32),
        "conv_bias": centred(arg_keys[2], (C,), 0.5, 3.0, (), jnp.float32),
        "spectral_weight": centred(arg_keys[3], (MODES, 2 * C * C), 2.0, 12.0, ((0, 512),), jnp.float32),
    }


highest = lax.Precision.HIGHEST

def contract(form, left, right):
    return jnp.einsum(form, left, right, precision=highest)

def mode_numbers(number, length):
    series = jnp.arange(number, dtype=jnp.int32)
    return jnp.where(series < number // 2, series, length - number + series)

def angles(places, mode_list, length):
    product = places[:, None] * mode_list[None, :] % length
    return 2.0 * math.pi / length * product.astype(jnp.float32)

def reference(features, conv_weight, conv_bias, spectral_weight):
    channels = features.shape[0]
    norm_factor = 1.0 / math.sqrt(NX * NY * NZ)
    deep_angle = angles(jnp.arange(NZ, dtype=jnp.int32), jnp.arange(KZ, dtype=jnp.int32), NZ)
    deep_cos = jnp.cos(deep_angle)
    deep_sin = jnp.sin(deep_angle)
    wide_angle = angles(jnp.arange(NY, dtype=jnp.int32), mode_numbers(KY, NY), NY)
    wide_cos = jnp.cos(wide_angle)
    wide_sin = jnp.sin(wide_angle)
    long_angle = angles(jnp.arange(NX, dtype=jnp.int32), mode_numbers(KX, NX), NX)
    long_cos = jnp.cos(long_angle)
    long_sin = jnp.sin(long_angle)
    deep_real = contract('cxyz,zk->cxyk', features, deep_cos)
    deep_imag = -contract('cxyz,zk->cxyk', features, deep_sin)
    wide_real = contract('cxyk,yb->cxbk', deep_real, wide_cos) + contract('cxyk,yb->cxbk', deep_imag, wide_sin)
    wide_imag = contract('cxyk,yb->cxbk', deep_imag, wide_cos) - contract('cxyk,yb->cxbk', deep_real, wide_sin)
    long_real = contract('cxbk,xa->bkac', wide_real, long_cos) + contract('cxbk,xa->bkac', wide_imag, long_sin)
    long_imag = contract('cxbk,xa->bkac', wide_imag, long_cos) - contract('cxbk,xa->bkac', wide_real, long_sin)
    hat_real = long_real.reshape(MODES, channels) * norm_factor
    hat_imag = long_imag.reshape(MODES, channels) * norm_factor
    weights = spectral_weight.reshape(MODES, 2, channels, channels)
    mixed_real = contract('mi,mio->mo', hat_real, weights[:, 0]) - contract('mi,mio->mo', hat_imag, weights[:, 1])
    mixed_imag = contract('mi,mio->mo', hat_real, weights[:, 1]) + contract('mi,mio->mo', hat_imag, weights[:, 0])
    mixed_real = mixed_real.reshape(PAIRS, KX, channels)
    mixed_imag = mixed_imag.reshape(PAIRS, KX, channels)
    back_real = contract('pao,xa->xpo', mixed_real, long_cos) - contract('pao,xa->xpo', mixed_imag, long_sin)
    back_imag = contract('pao,xa->xpo', mixed_real, long_sin) + contract('pao,xa->xpo', mixed_imag, long_cos)
    back_real = back_real.reshape(NX, KY, KZ, channels)
    back_imag = back_imag.reshape(NX, KY, KZ, channels)
    side_real = contract('xbko,yb->kxyo', back_real, wide_cos) - contract('xbko,yb->kxyo', back_imag, wide_sin)
    side_imag = contract('xbko,yb->kxyo', back_real, wide_sin) + contract('xbko,yb->kxyo', back_imag, wide_cos)
    factor = jnp.where(jnp.arange(KZ) == 0, 1.0, 2.0).astype(jnp.float32)
    spectral_term = norm_factor * (contract('kxyo,zk->oxyz', side_real, deep_cos * factor[None, :]) - contract('kxyo,zk->oxyz', side_imag, deep_sin * factor[None, :]))
    kernel = jnp.transpose(conv_weight, (4, 3, 0, 1, 2))
    local_term = lax.conv_general_dilated(features[None], kernel, (1, 1, 1), ((1, 1), (1, 1), (1, 1)), dimension_numbers=('NCDHW', 'OIDHW', 'NCDHW'), precision=highest)[0]
    return jax.nn.gelu(spectral_term + local_term + conv_bias[:, None, None, None], approximate=False)
```

```python
import math

import jax
import jax.numpy as jnp
from jax import lax
from jax.sharding import PartitionSpec as P

KX = 16
KY = 16
KZ = 16


highest = lax.Precision.HIGHEST


def extended(cells, sides, width):
    for axis, dim in sides:
        count = lax.axis_size(axis)
        ends = count - 1
        head = lax.slice_in_dim(cells, 0, width, axis=dim)
        tail = lax.slice_in_dim(cells, cells.shape[dim] - width, cells.shape[dim], axis=dim)
        cells = jnp.concatenate(
            [
                lax.ppermute(tail, axis, [(i, (i + 1) % count) for i in range(ends)]),
                cells,
                lax.ppermute(head, axis, [((i + 1) % count, i) for i in range(ends)]),
            ],
            axis=dim,
        )
    return cells


def contract(form, left, right):
    return jnp.einsum(form, left, right, precision=highest)


def mode_numbers(number, length):
    series = jnp.arange(number, dtype=jnp.int32)
    return jnp.where(series < number // 2, series, length - number + series)


def angles(places, mode_list, length):
    product = places[:, None] * mode_list[None, :] % length
    return 2.0 * math.pi / length * product.astype(jnp.float32)


def receive_modes(rows, long_cos, long_sin, channels):
    rows_real = rows[:, :channels]
    rows_imag = rows[:, channels:]
    hat_real = contract("xc,xa->ac", rows_real, long_cos) + contract(
        "xc,xa->ac", rows_imag, long_sin
    )
    hat_imag = contract("xc,xa->ac", rows_imag, long_cos) - contract(
        "xc,xa->ac", rows_real, long_sin
    )
    return (hat_real, hat_imag)


def mix_modes(hat_real, hat_imag, spectral_weight, channels):
    weights = spectral_weight.reshape(-1, 2, channels, channels)
    mixed_real = contract("mi,mio->mo", hat_real, weights[:, 0]) - contract(
        "mi,mio->mo", hat_imag, weights[:, 1]
    )
    mixed_imag = contract("mi,mio->mo", hat_real, weights[:, 1]) + contract(
        "mi,mio->mo", hat_imag, weights[:, 0]
    )
    return (mixed_real, mixed_imag)


def send_modes(mixed_real, mixed_imag, long_cos, long_sin):
    back_real = contract("ao,xa->xo", mixed_real, long_cos) - contract(
        "ao,xa->xo", mixed_imag, long_sin
    )
    back_imag = contract("ao,xa->xo", mixed_real, long_sin) + contract(
        "ao,xa->xo", mixed_imag, long_cos
    )
    return jnp.concatenate([back_real, back_imag], axis=1)


def local(features, conv_weight, conv_bias, spectral_weight):
    channels, rows_x, rows_y, depth = features.shape
    length_x = rows_x * lax.axis_size("gx")
    length_y = rows_y * lax.axis_size("gy")
    norm_factor = 1.0 / math.sqrt(length_x * length_y * depth)
    first_x = lax.axis_index("gx") * rows_x
    first_y = lax.axis_index("gy") * rows_y
    pairs = KY * KZ
    padded = extended(features, (("gx", 1), ("gy", 2)), 1)
    padded = jnp.pad(padded, ((0, 0), (0, 0), (0, 0), (1, 1)))
    local_term = jnp.zeros(features.shape, jnp.float32)
    for shift_x in range(3):
        for shift_y in range(3):
            for shift_z in range(3):
                window = padded[
                    :,
                    shift_x : shift_x + rows_x,
                    shift_y : shift_y + rows_y,
                    shift_z : shift_z + depth,
                ]
                local_term = local_term + contract(
                    "ixyz,io->oxyz", window, conv_weight[shift_x, shift_y, shift_z]
                )
    deep_angle = angles(jnp.arange(depth, dtype=jnp.int32), jnp.arange(KZ, dtype=jnp.int32), depth)
    deep_cos = jnp.cos(deep_angle)
    deep_sin = jnp.sin(deep_angle)
    wide_angle = angles(
        first_y + jnp.arange(rows_y, dtype=jnp.int32), mode_numbers(KY, length_y), length_y
    )
    wide_cos = jnp.cos(wide_angle)
    wide_sin = jnp.sin(wide_angle)
    deep_real = contract("cxyz,zk->cxyk", features, deep_cos)
    deep_imag = -contract("cxyz,zk->cxyk", features, deep_sin)
    wide_real = contract("cxyk,yb->xbkc", deep_real, wide_cos) + contract(
        "cxyk,yb->xbkc", deep_imag, wide_sin
    )
    wide_imag = contract("cxyk,yb->xbkc", deep_imag, wide_cos) - contract(
        "cxyk,yb->xbkc", deep_real, wide_sin
    )
    owners = ("gx", "gy")
    halves = lax.axis_size("gx") * lax.axis_size("gy") // pairs
    share = KX // halves
    outgoing = jnp.concatenate(
        [wide_real.reshape(pairs, channels), wide_imag.reshape(pairs, channels)], axis=1
    )
    outgoing = jnp.repeat(outgoing, halves, axis=0)
    arrived = lax.all_to_all(outgoing, owners, 0, 0, tiled=True)
    half = lax.axis_index("gy") % halves
    long_modes = lax.dynamic_slice_in_dim(mode_numbers(KX, length_x), half * share, share)
    places = jnp.repeat(jnp.arange(length_x, dtype=jnp.int32), lax.axis_size("gy"))
    long_angle = angles(places, long_modes, length_x)
    long_cos = jnp.cos(long_angle)
    long_sin = jnp.sin(long_angle)
    hat_real, hat_imag = receive_modes(arrived, long_cos, long_sin, channels)
    mixed_real, mixed_imag = mix_modes(
        hat_real * norm_factor, hat_imag * norm_factor, spectral_weight, channels
    )
    returning = send_modes(mixed_real, mixed_imag, long_cos, long_sin)
    whole = lax.all_to_all(returning, owners, 0, 0, tiled=True)
    whole = whole.reshape(pairs, halves, 2, channels).sum(axis=1)
    back_real = whole[:, 0].reshape(rows_x, KY, KZ, channels)
    back_imag = whole[:, 1].reshape(rows_x, KY, KZ, channels)
    side_real = contract("xbko,yb->kxyo", back_real, wide_cos) - contract(
        "xbko,yb->kxyo", back_imag, wide_sin
    )
    side_imag = contract("xbko,yb->kxyo", back_real, wide_sin) + contract(
        "xbko,yb->kxyo", back_imag, wide_cos
    )
    factor = jnp.where(jnp.arange(KZ) == 0, 1.0, 2.0).astype(jnp.float32)
    spectral_term = norm_factor * (
        contract("kxyo,zk->oxyz", side_real, deep_cos * factor[None, :])
        - contract("kxyo,zk->oxyz", side_imag, deep_sin * factor[None, :])
    )
    return jax.nn.gelu(
        spectral_term + local_term + conv_bias[:, None, None, None], approximate=False
    )


def solution(mesh):
    return jax.shard_map(
        local,
        mesh=mesh,
        in_specs=(P(None, "gx", "gy", None), P(), P(), P(("gx", "gy"), None)),
        out_specs=P(None, "gx", "gy", None),
        check_vma=False,
    )
```

```python
import math

import jax
import jax.numpy as jnp
import numpy as np
from jax import lax
from jax.experimental import pallas as pl
from jax.experimental.pallas import tpu as pltpu
from jax.sharding import PartitionSpec as P

KX = 16
KY = 16
KZ = 16
GROUP = 8
LANES = 128

f32 = jnp.float32
bf16 = jnp.bfloat16
highest = lax.Precision.HIGHEST


def halves_of(value):
    high = value.astype(bf16)
    return high, (value - high.astype(f32)).astype(bf16)


def fixed_halves(table):
    table = np.asarray(table, np.float32)
    high = table.astype(bf16)
    return jnp.asarray(high), jnp.asarray((table - high.astype(np.float32)).astype(bf16))


def product(left, right, dims):
    return lax.dot_general(left, right, (dims, ((), ())), preferred_element_type=f32)


def product_of_halves(left, right, dims):
    return (
        product(left[0], right[0], dims)
        + product(left[0], right[1], dims)
        + product(left[1], right[0], dims)
    )


def signed_modes(number):
    series = np.arange(number)
    return np.where(series < number // 2, series, series - number)


def forward_tables(rows_y, length_y, depth):
    angle = 2.0 * np.pi / length_y * np.outer(signed_modes(KY), np.arange(rows_y))
    same = np.eye(GROUP)
    wide = np.einsum("rby,ij->rbijy", np.stack([np.cos(angle), -np.sin(angle)]), same)
    wide = wide.reshape(2 * KY * GROUP, GROUP * rows_y)
    angle = 2.0 * np.pi / depth * np.outer(np.arange(KZ), np.arange(depth))
    deep_cos = np.cos(angle)
    deep_sin = np.sin(angle)
    deep = np.concatenate(
        [
            np.concatenate([deep_cos, deep_sin], axis=1),
            np.concatenate([-deep_sin, deep_cos], axis=1),
        ],
        axis=0,
    )
    return wide, deep


def inverse_tables(rows_y, length_y, depth, norm_factor):
    angle = 2.0 * np.pi / length_y * np.outer(np.arange(rows_y), signed_modes(KY))
    same = np.eye(GROUP)
    wide = np.einsum("ryb,ij->iyrbj", np.stack([np.cos(angle), -np.sin(angle)]), same)
    wide = wide.reshape(GROUP * rows_y, 2 * KY * GROUP)
    angle = 2.0 * np.pi / depth * np.outer(np.arange(KZ), np.arange(depth))
    factor = norm_factor * np.where(np.arange(KZ) == 0, 1.0, 2.0)[:, None]
    deep_cos = factor * np.cos(angle)
    deep_sin = factor * np.sin(angle)
    deep = np.concatenate(
        [
            np.concatenate([deep_cos, deep_sin], axis=1),
            np.concatenate([-deep_sin, deep_cos], axis=1),
        ],
        axis=0,
    )
    return wide, deep


def forward_kernel(
    cells_ref, wide_high, wide_low, deep_high, deep_low, out_ref, middle_ref, pair_ref
):
    channels = middle_ref.shape[0] // KY
    block = wide_high.shape[1]
    groups = channels // GROUP
    wide = (wide_high[...], wide_low[...])
    for first in range(0, groups, 2):
        cells = jnp.concatenate(
            [
                cells_ref[first * block : (first + 1) * block, :],
                cells_ref[(first + 1) * block : (first + 2) * block, :],
            ],
            axis=1,
        )
        summed = product_of_halves(wide, halves_of(cells), ((1,), (0,)))
        for part in range(2):
            for mode in range(KY):
                row = (part * KY + mode) * GROUP
                for side in range(2):
                    place = mode * channels + (first + side) * GROUP
                    middle_ref[place : place + GROUP, part * LANES : (part + 1) * LANES] = (
                        summed[row : row + GROUP, side * LANES : (side + 1) * LANES]
                    )
    modes = product_of_halves(
        (deep_high[...], deep_low[...]), halves_of(middle_ref[...]), ((1,), (1,))
    )
    pair_ref[...] = jnp.zeros_like(pair_ref)
    for mode in range(KY):
        first = mode * channels
        for part in range(2):
            pair_ref[mode * KZ : (mode + 1) * KZ, part * channels : (part + 1) * channels] = (
                modes[part * KZ : (part + 1) * KZ, first : first + channels]
            )
    pairs = pair_ref[...]
    out_ref[pl.ds(0, KY * KZ, stride=2), :] = pairs
    out_ref[pl.ds(1, KY * KZ, stride=2), :] = pairs


def middle_kernel(rows_ref, basis_ref, weight_ref, out_ref, *, channels, norm_factor):
    basis = basis_ref[...]
    share = basis.shape[0] // 2
    sums = norm_factor * jnp.dot(
        basis, rows_ref[...], precision=highest, preferred_element_type=f32
    )
    hat_real = sums[:share, :channels] + sums[share:, channels : 2 * channels]
    hat_imag = sums[:share, channels : 2 * channels] - sums[share:, :channels]
    size = channels * channels
    lane = lax.broadcasted_iota(jnp.int32, (channels, size), 1)
    row = lax.broadcasted_iota(jnp.int32, (channels, size), 0)
    spread = jnp.where(lane // channels == row, 1.0, 0.0).astype(f32)
    hat = jnp.dot(
        jnp.concatenate([hat_real, hat_imag], axis=0),
        spread,
        precision=highest,
        preferred_element_type=f32,
    )
    real = hat[:share]
    imag = hat[share:]
    weight_real = weight_ref[:, :size]
    weight_imag = weight_ref[:, size:]
    terms = jnp.concatenate(
        [real * weight_real - imag * weight_imag, real * weight_imag + imag * weight_real], axis=0
    )
    mixed = terms[:, :LANES]
    for start in range(LANES, size, LANES):
        mixed = mixed + terms[:, start : start + LANES]
    step = LANES // 2
    while step >= channels:
        mixed = mixed + pltpu.roll(mixed, step, axis=1)
        step = step // 2
    lane = lax.broadcasted_iota(jnp.int32, (share, LANES), 1)
    mixed_real = mixed[:share]
    mixed_imag = mixed[share:]
    stacked = jnp.concatenate(
        [
            jnp.where(lane < channels, mixed_real, mixed_imag),
            jnp.where(lane < channels, -mixed_imag, mixed_real),
        ],
        axis=0,
    )
    out_ref[...] = lax.dot_general(
        basis, stacked, (((0,), (0,)), ((), ())), precision=highest, preferred_element_type=f32
    )


def edges_kernel(left_ref, cells_ref, right_ref, tails_ref, heads_ref, *, rows_y, channels):
    planes = (left_ref, cells_ref, right_ref)
    for plane in range(3):
        rows = pl.ds(plane * channels, channels)
        heads_ref[rows, :] = planes[plane][pl.ds(0, channels, stride=rows_y), :]
        tails_ref[rows, :] = planes[plane][pl.ds(rows_y - 1, channels, stride=rows_y), :]


def doubled_taps(taps):
    high, low = halves_of(taps)
    return jnp.concatenate([high, high, low], axis=1)


def doubled_cells(cells):
    high, low = halves_of(cells)
    return jnp.concatenate([high, low, high], axis=0)


def shifted_sum(parts, depth):
    lane = lax.broadcasted_iota(jnp.int32, parts[1].shape, 1)
    below = jnp.where(lane == 0, 0.0, pltpu.roll(parts[0], 1, axis=1))
    above = jnp.where(lane == depth - 1, 0.0, pltpu.roll(parts[2], depth - 1, axis=1))
    return parts[1] + below + above


def conv_kernel(
    left_ref, cells_ref, right_ref, taps_ref, bias_ref, out_ref, taps_scratch, sums_scratch,
    *, rows_y, channels, depth
):
    planes = (left_ref, cells_ref, right_ref)
    width = 3 * channels
    taps_scratch[...] = doubled_taps(taps_ref[...])
    sums_scratch[0, :width, :] = jnp.zeros((width, depth), f32)
    sums_scratch[rows_y + 1, 2 * width :, :] = jnp.zeros((width, depth), f32)

    def row_cells(row):
        return jnp.concatenate(
            [plane[pl.ds(row, channels, stride=rows_y), :] for plane in planes], axis=0
        )

    def multiply(step, _):
        cells = jnp.concatenate([row_cells(2 * step), row_cells(2 * step + 1)], axis=1)
        sums = product(taps_scratch[...], doubled_cells(cells), ((1,), (0,)))
        sums_scratch[2 * step + 1] = sums[:, :depth]
        sums_scratch[2 * step + 2] = sums[:, depth:]
        return 0

    lax.fori_loop(0, rows_y // 2, multiply, 0)
    bias = bias_ref[...]

    def collect(row, _):
        parts = []
        for shift in range(3):
            first = shift * channels
            parts.append(
                sums_scratch[row, first : first + channels, :]
                + sums_scratch[row + 1, width + first : width + first + channels, :]
                + sums_scratch[row + 2, 2 * width + first : 2 * width + first + channels, :]
            )
        out_ref[pl.ds(row, channels, stride=rows_y), :] = shifted_sum(parts, depth) + bias
        return 0

    lax.fori_loop(0, rows_y, collect, 0)


def inverse_kernel(
    rows_ref, wide_high, wide_low, deep_high, deep_low, conv_ref, before_ref, after_ref, taps_ref,
    out_ref, modes_ref, middle_ref, conv_scratch, *, rows_y
):
    pairs = rows_ref[pl.ds(0, KY * KZ, stride=2), :] + rows_ref[pl.ds(1, KY * KZ, stride=2), :]
    channels = modes_ref.shape[1] // KY
    groups = channels // GROUP
    depth = conv_ref.shape[1]
    width = 3 * channels
    conv_scratch[...] = conv_ref[...]
    taps = jnp.concatenate([taps_ref[:width, :], taps_ref[2 * width :, :]], axis=0)
    cells = jnp.concatenate([before_ref[...], after_ref[...]], axis=1)
    sums = product(doubled_taps(taps), doubled_cells(cells), ((1,), (0,)))
    for row, values in ((0, sums[:width, :depth]), (rows_y - 1, sums[width:, depth:])):
        place = pl.ds(row, channels, stride=rows_y)
        parts = [values[r * channels : (r + 1) * channels] for r in range(3)]
        conv_scratch[place, :] = conv_scratch[place, :] + shifted_sum(parts, depth)
    for mode in range(KY):
        for part in range(2):
            modes_ref[part * KZ : (part + 1) * KZ, mode * channels : (mode + 1) * channels] = pairs[
                mode * KZ : (mode + 1) * KZ, part * channels : (part + 1) * channels
            ]
    deep = product_of_halves(
        halves_of(modes_ref[...]), (deep_high[...], deep_low[...]), ((0,), (0,))
    )
    for group in range(groups):
        for part in range(2):
            for mode in range(KY):
                row = (part * KY + mode) * GROUP
                place = mode * channels + group * GROUP
                middle_ref[row : row + GROUP, group * LANES : (group + 1) * LANES] = deep[
                    place : place + GROUP, part * LANES : (part + 1) * LANES
                ]
    wide = (wide_high[...], wide_low[...])
    block = wide_high.shape[0]
    for first in range(0, groups, 2):
        summed = product_of_halves(
            wide,
            halves_of(middle_ref[:, first * LANES : (first + 2) * LANES]),
            ((1,), (0,)),
        )
        for side in range(2):
            start = (first + side) * block
            value = (
                summed[:, side * LANES : (side + 1) * LANES] + conv_scratch[start : start + block, :]
            )
            out_ref[start : start + block, :] = (
                0.5 * value * (1.0 + lax.erf(value * math.sqrt(0.5)))
            )


def local(features, conv_weight, conv_bias, spectral_weight):
    channels, rows_x, rows_y, depth = features.shape
    count_x = lax.axis_size("gx")
    count_y = lax.axis_size("gy")
    length_x = rows_x * count_x
    length_y = rows_y * count_y
    norm_factor = 1.0 / math.sqrt(length_x * length_y * depth)
    pairs = KY * KZ
    owners = ("gx", "gy")
    devices = count_x * count_y
    halves = devices // pairs
    share = KX // halves
    params = pltpu.CompilerParams(vmem_limit_bytes=48 * 1024 * 1024)
    cells = features.reshape(channels * rows_y, depth)

    left = lax.ppermute(features, "gx", [(i, i + 1) for i in range(count_x - 1)])
    right = lax.ppermute(features, "gx", [(i + 1, i) for i in range(count_x - 1)])
    left = left.reshape(cells.shape)
    right = right.reshape(cells.shape)
    edge = jax.ShapeDtypeStruct((3 * channels, depth), f32)
    tails, heads = pl.pallas_call(
        lambda *refs: edges_kernel(*refs, rows_y=rows_y, channels=channels),
        out_shape=(edge, edge),
        compiler_params=params,
        name="edges",
    )(left, cells, right)
    before = lax.ppermute(tails, "gy", [(i, i + 1) for i in range(count_y - 1)])
    after = lax.ppermute(heads, "gy", [(i + 1, i) for i in range(count_y - 1)])

    wide, deep = forward_tables(rows_y, length_y, depth)
    outgoing = pl.pallas_call(
        forward_kernel,
        out_shape=jax.ShapeDtypeStruct((devices, LANES), f32),
        scratch_shapes=[
            pltpu.VMEM((KY * channels, 2 * depth), f32),
            pltpu.VMEM((pairs, LANES), f32),
        ],
        compiler_params=params,
        name="forward",
    )(cells, *fixed_halves(wide), *fixed_halves(deep))
    arrived = lax.all_to_all(outgoing, owners, 0, 0, tiled=True)

    device = lax.axis_index("gx") * count_y + lax.axis_index("gy")
    long_modes = device % halves * share + jnp.arange(share, dtype=jnp.int32)
    long_modes = jnp.where(long_modes < KX // 2, long_modes, length_x - KX + long_modes)
    wide_mode = device // halves // KZ
    wide_mode = jnp.where(wide_mode < KY // 2, wide_mode, length_y - KY + wide_mode)
    places = jnp.arange(devices, dtype=jnp.int32)
    steps = length_y // length_x * (long_modes[:, None] * (places // count_y)[None, :])
    steps = (steps + wide_mode * rows_y * (places % count_y)[None, :]) % length_y
    angle = 2.0 * math.pi / length_y * steps.astype(f32)
    basis = jnp.concatenate([jnp.cos(angle), jnp.sin(angle)], axis=0)
    returning = pl.pallas_call(
        lambda *refs: middle_kernel(*refs, channels=channels, norm_factor=norm_factor),
        out_shape=jax.ShapeDtypeStruct((devices, LANES), f32),
        compiler_params=params,
        name="middle",
    )(arrived, basis, spectral_weight)
    whole = lax.all_to_all(returning, owners, 0, 0, tiled=True)

    taps = jnp.transpose(conv_weight, (1, 2, 4, 0, 3)).reshape(9 * channels, 3 * channels)
    local_term = pl.pallas_call(
        lambda *refs: conv_kernel(*refs, rows_y=rows_y, channels=channels, depth=depth),
        out_shape=jax.ShapeDtypeStruct((channels * rows_y, depth), f32),
        scratch_shapes=[
            pltpu.VMEM((9 * channels, 9 * channels), bf16),
            pltpu.VMEM((rows_y + 2, 9 * channels, depth), f32),
        ],
        compiler_params=params,
        name="conv",
    )(left, cells, right, taps, jnp.broadcast_to(conv_bias[:, None], (channels, depth)))

    wide, deep = inverse_tables(rows_y, length_y, depth, norm_factor)
    layer_out = pl.pallas_call(
        lambda *refs: inverse_kernel(*refs, rows_y=rows_y),
        out_shape=jax.ShapeDtypeStruct((channels * rows_y, depth), f32),
        scratch_shapes=[
            pltpu.VMEM((2 * KZ, KY * channels), f32),
            pltpu.VMEM((2 * KY * GROUP, channels // GROUP * LANES), f32),
            pltpu.VMEM((channels * rows_y, depth), f32),
        ],
        compiler_params=params,
        name="inverse",
    )(whole, *fixed_halves(wide), *fixed_halves(deep), local_term, before, after, taps)
    return layer_out.reshape(features.shape)


def solution(mesh):
    return jax.shard_map(
        local,
        mesh=mesh,
        in_specs=(P(None, "gx", "gy", None), P(), P(), P(("gx", "gy"), None)),
        out_specs=P(None, "gx", "gy", None),
        check_vma=False,
    )
```

```python
import math

import jax
import jax.numpy as jnp
import numpy as np
from jax import lax
from jax.experimental import pallas as pl
from jax.experimental.pallas import tpu as pltpu
from jax.sharding import PartitionSpec as P

KX = 16
KY = 16
KZ = 16
GROUP = 8
LANES = 128

f32 = jnp.float32
bf16 = jnp.bfloat16
highest = lax.Precision.HIGHEST


def halves_of(value):
    high = value.astype(bf16)
    return high, (value - high.astype(f32)).astype(bf16)


def fixed_halves(table):
    table = np.asarray(table, np.float32)
    high = table.astype(bf16)
    return jnp.asarray(high), jnp.asarray((table - high.astype(np.float32)).astype(bf16))


def product(left, right, dims):
    return lax.dot_general(left, right, (dims, ((), ())), preferred_element_type=f32)


def product_of_halves(left, right, dims):
    return (
        product(left[0], right[0], dims)
        + product(left[0], right[1], dims)
        + product(left[1], right[0], dims)
    )


def signed_modes(number):
    series = np.arange(number)
    return np.where(series < number // 2, series, series - number)


def deep_angles(depth):
    order = np.concatenate([np.arange(0, KZ, 2), np.arange(1, KZ, 2)])
    return order, 2.0 * np.pi / depth * np.outer(order, np.arange(depth))


def forward_tables(rows_y, length_y, depth):
    angle = 2.0 * np.pi / length_y * np.outer(signed_modes(KY), np.arange(rows_y))
    same = np.eye(GROUP)
    wide = np.einsum("rby,ij->rbijy", np.stack([np.cos(angle), -np.sin(angle)]), same)
    wide = wide.reshape(2 * KY * GROUP, GROUP * rows_y)
    _, angle = deep_angles(depth)
    deep_cos = np.cos(angle)
    deep_sin = np.sin(angle)
    deep = np.concatenate(
        [
            np.concatenate([deep_cos, deep_sin], axis=1),
            np.concatenate([-deep_sin, deep_cos], axis=1),
        ],
        axis=0,
    )
    return wide, deep


def inverse_tables(rows_y, length_y, depth, norm_factor):
    angle = 2.0 * np.pi / length_y * np.outer(np.arange(rows_y), signed_modes(KY))
    same = np.eye(GROUP)
    wide = np.einsum("ryb,ij->iyrbj", np.stack([np.cos(angle), -np.sin(angle)]), same)
    wide = wide.reshape(GROUP * rows_y, 2 * KY * GROUP)
    order, angle = deep_angles(depth)
    factor = norm_factor * np.where(order == 0, 1.0, 2.0)[:, None]
    deep_cos = factor * np.cos(angle)
    deep_sin = factor * np.sin(angle)
    deep = np.concatenate(
        [
            np.concatenate([deep_cos, deep_sin], axis=1),
            np.concatenate([-deep_sin, deep_cos], axis=1),
        ],
        axis=0,
    )
    return wide, deep


def forward_kernel(
    cells_hbm, wide_high_hbm, wide_low_hbm, deep_high_hbm, deep_low_hbm, out_ref,
    cells_ref, wide_high, wide_low, deep_high, deep_low, middle_ref, sems
):
    half = cells_ref.shape[0] // 2
    chunks = [pl.ds(0, half), pl.ds(half, half)]
    moves = [
        (wide_high_hbm, wide_high),
        (wide_low_hbm, wide_low),
        (cells_hbm.at[chunks[0]], cells_ref.at[chunks[0]]),
        (cells_hbm.at[chunks[1]], cells_ref.at[chunks[1]]),
        (deep_high_hbm, deep_high),
        (deep_low_hbm, deep_low),
    ]
    copies = [pltpu.make_async_copy(*pair, sems.at[i]) for i, pair in enumerate(moves)]
    for copy in copies:
        copy.start()
    for copy in copies[:3]:
        copy.wait()
    channels = middle_ref.shape[0] // KY
    block = wide_high.shape[1]
    groups = channels // GROUP
    wide = (wide_high[...], wide_low[...])
    for first in range(0, groups, 2):
        if first == groups // 2:
            copies[3].wait()
        cells = jnp.concatenate(
            [
                cells_ref[first * block : (first + 1) * block, :],
                cells_ref[(first + 1) * block : (first + 2) * block, :],
            ],
            axis=1,
        )
        summed = product_of_halves(wide, halves_of(cells), ((1,), (0,)))
        for part in range(2):
            for mode in range(KY):
                row = (part * KY + mode) * GROUP
                for side in range(2):
                    place = mode * channels + (first + side) * GROUP
                    middle_ref[place : place + GROUP, part * LANES : (part + 1) * LANES] = (
                        summed[row : row + GROUP, side * LANES : (side + 1) * LANES]
                    )
    copies[4].wait()
    copies[5].wait()
    modes = product_of_halves(
        (deep_high[...], deep_low[...]), halves_of(middle_ref[...]), ((1,), (1,))
    )
    for mode in range(KY):
        for part in range(2):
            for odd in range(2):
                lane = odd * 2 * channels + part * channels
                row = (part * 2 + odd) * (KZ // 2)
                out_ref[mode * KZ // 2 : (mode + 1) * KZ // 2, lane : lane + channels] = modes[
                    row : row + KZ // 2, mode * channels : (mode + 1) * channels
                ]


def crossed(value, channels, sign):
    lane = lax.broadcasted_iota(jnp.int32, value.shape, 1)
    width = value.shape[1]
    return jnp.where(
        lane % (2 * channels) < channels,
        sign * pltpu.roll(value, width - channels, axis=1),
        -sign * pltpu.roll(value, channels, axis=1),
    )


def gather_kernel(rows_ref, basis_ref, out_ref, *, channels, share):
    length = basis_ref.shape[1]
    cells = jnp.concatenate(
        [rows_ref[pl.ds(0, length, stride=2), :], rows_ref[pl.ds(1, length, stride=2), :]], axis=1
    )
    sums = jnp.dot(basis_ref[...], cells, precision=highest, preferred_element_type=f32)
    for tile in range(2):
        lanes = slice(tile * LANES, (tile + 1) * LANES)
        modes = sums[:KX, lanes] + crossed(sums[KX:, lanes], channels, 1.0)
        start = 2 * tile * KX
        out_ref[start : start + KX, :] = modes
        out_ref[start + KX : start + 2 * KX, :] = pltpu.roll(modes, LANES // 2, axis=1)


def spread_kernel(rows_ref, basis_ref, out_ref, *, channels):
    length = basis_ref.shape[1]
    for tile in range(2):
        start = 2 * tile * KX
        even = rows_ref[start : start + KX, :]
        odd = pltpu.roll(rows_ref[start + KX : start + 2 * KX, :], LANES // 2, axis=1)
        lane = lax.broadcasted_iota(jnp.int32, even.shape, 1)
        modes = jnp.where(lane < LANES // 2, even, odd)
        both = jnp.concatenate([modes, crossed(modes, channels, -1.0)], axis=0)
        out_ref[pl.ds(tile, length, stride=2), :] = lax.dot_general(
            basis_ref[...],
            both,
            (((0,), (0,)), ((), ())),
            precision=highest,
            preferred_element_type=f32,
        )


def middle_kernel(rows_ref, weight_ref, out_ref, *, channels, norm_factor):
    share = weight_ref.shape[0]
    sums = rows_ref[:share, :]
    for start in range(share, rows_ref.shape[0], share):
        sums = sums + rows_ref[start : start + share, :]
    sums = norm_factor * sums
    hat_real = sums[:, :channels]
    hat_imag = sums[:, channels : 2 * channels]
    size = channels * channels
    lane = lax.broadcasted_iota(jnp.int32, (channels, size), 1)
    row = lax.broadcasted_iota(jnp.int32, (channels, size), 0)
    spread = jnp.where(lane // channels == row, 1.0, 0.0).astype(f32)
    hat = jnp.dot(
        jnp.concatenate([hat_real, hat_imag], axis=0),
        spread,
        precision=highest,
        preferred_element_type=f32,
    )
    real = hat[:share]
    imag = hat[share:]
    weight_real = weight_ref[:, :size]
    weight_imag = weight_ref[:, size:]
    terms = jnp.concatenate(
        [real * weight_real - imag * weight_imag, real * weight_imag + imag * weight_real], axis=0
    )
    mixed = terms[:, :LANES]
    for start in range(LANES, size, LANES):
        mixed = mixed + terms[:, start : start + LANES]
    step = LANES // 2
    while step >= channels:
        mixed = mixed + pltpu.roll(mixed, step, axis=1)
        step = step // 2
    lane = lax.broadcasted_iota(jnp.int32, (share, LANES), 1)
    mixed_real = mixed[:share]
    mixed_imag = mixed[share:]
    mixed = jnp.where(lane < channels, mixed_real, mixed_imag)
    for start in range(0, out_ref.shape[0], share):
        out_ref[start : start + share, :] = mixed


def edges_kernel(left_ref, cells_ref, right_ref, tails_ref, heads_ref, *, rows_y, channels):
    planes = (left_ref, cells_ref, right_ref)
    for plane in range(3):
        rows = pl.ds(plane * channels, channels)
        heads_ref[rows, :] = planes[plane][pl.ds(0, channels, stride=rows_y), :]
        tails_ref[rows, :] = planes[plane][pl.ds(rows_y - 1, channels, stride=rows_y), :]


def doubled_taps(taps):
    high, low = halves_of(taps)
    return jnp.concatenate([high, high, low], axis=1)


def doubled_cells(cells):
    high, low = halves_of(cells)
    return jnp.concatenate([high, low, high], axis=0)


def shifted_sum(parts, depth):
    lane = lax.broadcasted_iota(jnp.int32, parts[1].shape, 1)
    below = jnp.where(lane == 0, 0.0, pltpu.roll(parts[0], 1, axis=1))
    above = jnp.where(lane == depth - 1, 0.0, pltpu.roll(parts[2], depth - 1, axis=1))
    return parts[1] + below + above


def conv_kernel(*refs, planes, rows_y, channels, depth):
    plane_refs = refs[: len(planes)]
    taps_ref, base_ref, out_ref, sums_scratch = refs[len(planes) :]
    width = 3 * channels
    taps = jnp.concatenate(
        [taps_ref[:, plane * channels : (plane + 1) * channels] for plane in planes], axis=1
    )
    taps = doubled_taps(taps)
    sums_scratch[0, :width, :] = jnp.zeros((width, depth), f32)
    sums_scratch[rows_y + 1, 2 * width :, :] = jnp.zeros((width, depth), f32)

    def row_cells(row):
        return jnp.concatenate(
            [plane[pl.ds(row, channels, stride=rows_y), :] for plane in plane_refs], axis=0
        )

    def collect(row):
        parts = []
        for shift in range(3):
            first = shift * channels
            parts.append(
                sums_scratch[row, first : first + channels, :]
                + sums_scratch[row + 1, width + first : width + first + channels, :]
                + sums_scratch[row + 2, 2 * width + first : 2 * width + first + channels, :]
            )
        place = pl.ds(row, channels, stride=rows_y)
        base = base_ref[place, :] if base_ref.shape == out_ref.shape else base_ref[...]
        out_ref[place, :] = shifted_sum(parts, depth) + base

    for step in range(rows_y // 2):
        cells = jnp.concatenate([row_cells(2 * step), row_cells(2 * step + 1)], axis=1)
        sums = product(taps, doubled_cells(cells), ((1,), (0,)))
        sums_scratch[2 * step + 1] = sums[:, :depth]
        sums_scratch[2 * step + 2] = sums[:, depth:]
        if step:
            collect(2 * step - 2)
            collect(2 * step - 1)
    collect(rows_y - 2)
    collect(rows_y - 1)


def inverse_kernel(
    rows_ref, wide_high, wide_low, deep_high, deep_low, conv_ref, before_ref, after_ref, taps_ref,
    out_ref, modes_ref, middle_ref, conv_scratch, *, rows_y
):
    channels = modes_ref.shape[1] // KY
    groups = channels // GROUP
    depth = conv_ref.shape[1]
    width = 3 * channels
    conv_scratch[...] = conv_ref[...]
    taps = jnp.concatenate([taps_ref[:width, :], taps_ref[2 * width :, :]], axis=0)
    cells = jnp.concatenate([before_ref[...], after_ref[...]], axis=1)
    sums = product(doubled_taps(taps), doubled_cells(cells), ((1,), (0,)))
    for row, values in ((0, sums[:width, :depth]), (rows_y - 1, sums[width:, depth:])):
        place = pl.ds(row, channels, stride=rows_y)
        parts = [values[r * channels : (r + 1) * channels] for r in range(3)]
        conv_scratch[place, :] = conv_scratch[place, :] + shifted_sum(parts, depth)
    for mode in range(KY):
        for part in range(2):
            for odd in range(2):
                lane = odd * 2 * channels + part * channels
                row = (part * 2 + odd) * (KZ // 2)
                modes_ref[row : row + KZ // 2, mode * channels : (mode + 1) * channels] = rows_ref[
                    mode * KZ // 2 : (mode + 1) * KZ // 2, lane : lane + channels
                ]
    deep = product_of_halves(
        halves_of(modes_ref[...]), (deep_high[...], deep_low[...]), ((0,), (0,))
    )
    for group in range(groups):
        for part in range(2):
            for mode in range(KY):
                row = (part * KY + mode) * GROUP
                place = mode * channels + group * GROUP
                middle_ref[row : row + GROUP, group * LANES : (group + 1) * LANES] = deep[
                    place : place + GROUP, part * LANES : (part + 1) * LANES
                ]
    wide = (wide_high[...], wide_low[...])
    block = wide_high.shape[0]
    for first in range(0, groups, 2):
        summed = product_of_halves(
            wide,
            halves_of(middle_ref[:, first * LANES : (first + 2) * LANES]),
            ((1,), (0,)),
        )
        for side in range(2):
            start = (first + side) * block
            value = (
                summed[:, side * LANES : (side + 1) * LANES] + conv_scratch[start : start + block, :]
            )
            out_ref[start : start + block, :] = (
                0.5 * value * (1.0 + lax.erf(value * math.sqrt(0.5)))
            )


def local(features, conv_weight, conv_bias, spectral_weight):
    channels, rows_x, rows_y, depth = features.shape
    count_x = lax.axis_size("gx")
    count_y = lax.axis_size("gy")
    length_x = rows_x * count_x
    length_y = rows_y * count_y
    norm_factor = 1.0 / math.sqrt(length_x * length_y * depth)
    pairs = KY * KZ
    devices = count_x * count_y
    halves = devices // pairs
    share = KX // halves
    params = pltpu.CompilerParams(vmem_limit_bytes=48 * 1024 * 1024)
    cells = features.reshape(channels * rows_y, depth)

    wide, deep = forward_tables(rows_y, length_y, depth)
    outgoing = pl.pallas_call(
        forward_kernel,
        out_shape=jax.ShapeDtypeStruct((pairs // 2, LANES), f32),
        in_specs=[pl.BlockSpec(memory_space=pltpu.HBM)] * 5,
        scratch_shapes=[
            pltpu.VMEM(cells.shape, f32),
            pltpu.VMEM(wide.shape, bf16),
            pltpu.VMEM(wide.shape, bf16),
            pltpu.VMEM(deep.shape, bf16),
            pltpu.VMEM(deep.shape, bf16),
            pltpu.VMEM((KY * channels, 2 * depth), f32),
            pltpu.SemaphoreType.DMA((6,)),
        ],
        compiler_params=params,
        name="forward",
    )(cells, *fixed_halves(wide), *fixed_halves(deep))
    taps = jnp.transpose(conv_weight, (1, 2, 4, 0, 3)).reshape(9 * channels, 3 * channels)
    bias = jnp.broadcast_to(conv_bias[:, None], (channels, depth))

    def conv(name, planes, *operands):
        return pl.pallas_call(
            lambda *refs: conv_kernel(
                *refs, planes=planes, rows_y=rows_y, channels=channels, depth=depth
            ),
            out_shape=jax.ShapeDtypeStruct(cells.shape, f32),
            scratch_shapes=[pltpu.VMEM((rows_y + 2, 9 * channels, depth), f32)],
            compiler_params=params,
            name=name,
        )(*operands)

    left = lax.ppermute(features, "gx", [(i, i + 1) for i in range(count_x - 1)])
    right = lax.ppermute(features, "gx", [(i + 1, i) for i in range(count_x - 1)])
    left = left.reshape(cells.shape)
    right = right.reshape(cells.shape)
    edge = jax.ShapeDtypeStruct((3 * channels, depth), f32)
    tails, heads = pl.pallas_call(
        lambda *refs: edges_kernel(*refs, rows_y=rows_y, channels=channels),
        out_shape=(edge, edge),
        compiler_params=params,
        name="edges",
    )(left, cells, right)
    before = lax.ppermute(tails, "gy", [(i, i + 1) for i in range(count_y - 1)])
    after = lax.ppermute(heads, "gy", [(i + 1, i) for i in range(count_y - 1)])
    local_term = conv("conv", (0, 1, 2), left, cells, right, taps, bias)

    long_modes = jnp.arange(KX, dtype=jnp.int32)
    long_modes = jnp.where(long_modes < KX // 2, long_modes, length_x - KX + long_modes)
    wide_mode = lax.axis_index("gx") * pairs // count_x // KZ
    wide_mode = jnp.where(wide_mode < KY // 2, wide_mode, length_y - KY + wide_mode)
    places = jnp.arange(length_x, dtype=jnp.int32)
    steps = length_y // length_x * (long_modes[:, None] * places[None, :])
    steps = (steps + wide_mode * rows_y * lax.axis_index("gy")) % length_y
    angle = 2.0 * math.pi / length_y * steps.astype(f32)
    basis = jnp.concatenate([jnp.cos(angle), jnp.sin(angle)], axis=0)

    def small(kernel, name, rows, *operands):
        return pl.pallas_call(
            kernel,
            out_shape=jax.ShapeDtypeStruct((rows, LANES), f32),
            compiler_params=params,
            name=name,
        )(*operands)

    arrived = lax.all_to_all(outgoing, "gx", 0, 0, tiled=True)
    partial_modes = small(
        lambda *refs: gather_kernel(*refs, channels=channels, share=share),
        "gather", count_y * share, arrived, basis,
    )
    owned = lax.all_to_all(partial_modes, "gy", 0, 0, tiled=True)
    mixed = small(
        lambda *refs: middle_kernel(*refs, channels=channels, norm_factor=norm_factor),
        "middle", count_y * share, owned, spectral_weight,
    )
    shared = lax.all_to_all(mixed, "gy", 0, 0, tiled=True)
    returning = small(
        lambda *refs: spread_kernel(*refs, channels=channels),
        "spread", pairs // 2, shared, basis,
    )
    whole = lax.all_to_all(returning, "gx", 0, 0, tiled=True)

    wide, deep = inverse_tables(rows_y, length_y, depth, norm_factor)
    layer_out = pl.pallas_call(
        lambda *refs: inverse_kernel(*refs, rows_y=rows_y),
        out_shape=jax.ShapeDtypeStruct((channels * rows_y, depth), f32),
        scratch_shapes=[
            pltpu.VMEM((2 * KZ, KY * channels), f32),
            pltpu.VMEM((2 * KY * GROUP, channels // GROUP * LANES), f32),
            pltpu.VMEM((channels * rows_y, depth), f32),
        ],
        compiler_params=params,
        name="inverse",
    )(whole, *fixed_halves(wide), *fixed_halves(deep), local_term, before, after, taps)
    return layer_out.reshape(features.shape)


def solution(mesh):
    return jax.shard_map(
        local,
        mesh=mesh,
        in_specs=(P(None, "gx", "gy", None), P(), P(), P(("gx", "gy"), None)),
        out_specs=P(None, "gx", "gy", None),
        check_vma=False,
    )
```

```python
import math

import jax
import jax.numpy as jnp
import numpy as np
from jax import lax
from jax.experimental import pallas as pl
from jax.experimental.pallas import tpu as pltpu
from jax.sharding import PartitionSpec as P

KX = 16
KY = 16
KZ = 16
GROUP = 8
LANES = 128

f32 = jnp.float32
bf16 = jnp.bfloat16
highest = lax.Precision.HIGHEST


def halves_of(value):
    high = value.astype(bf16)
    return high, (value - high.astype(f32)).astype(bf16)


def fixed_halves(table):
    table = np.asarray(table, np.float32)
    high = table.astype(bf16)
    return jnp.asarray(high), jnp.asarray((table - high.astype(np.float32)).astype(bf16))


def product(left, right, dims):
    return lax.dot_general(left, right, (dims, ((), ())), preferred_element_type=f32)


def product_of_halves(left, right, dims):
    return (
        product(left[0], right[0], dims)
        + product(left[0], right[1], dims)
        + product(left[1], right[0], dims)
    )


def signed_modes(number):
    series = np.arange(number)
    return np.where(series < number // 2, series, series - number)


def deep_angles(depth):
    order = np.concatenate([np.arange(0, KZ, 2), np.arange(1, KZ, 2)])
    return order, 2.0 * np.pi / depth * np.outer(order, np.arange(depth))


def forward_tables(rows_y, length_y, depth):
    angle = 2.0 * np.pi / length_y * np.outer(signed_modes(KY), np.arange(rows_y))
    same = np.eye(GROUP)
    wide = np.einsum("rby,ij->rbijy", np.stack([np.cos(angle), -np.sin(angle)]), same)
    wide = wide.reshape(2 * KY * GROUP, GROUP * rows_y)
    _, angle = deep_angles(depth)
    deep_cos = np.cos(angle)
    deep_sin = np.sin(angle)
    deep = np.concatenate(
        [
            np.concatenate([deep_cos, deep_sin], axis=1),
            np.concatenate([-deep_sin, deep_cos], axis=1),
        ],
        axis=0,
    )
    return wide, deep


def inverse_tables(rows_y, length_y, depth, norm_factor):
    angle = 2.0 * np.pi / length_y * np.outer(np.arange(rows_y), signed_modes(KY))
    same = np.eye(GROUP)
    wide = np.einsum("ryb,ij->iyrbj", np.stack([np.cos(angle), -np.sin(angle)]), same)
    wide = wide.reshape(GROUP * rows_y, 2 * KY * GROUP)
    order, angle = deep_angles(depth)
    factor = norm_factor * np.where(order == 0, 1.0, 2.0)[:, None]
    deep_cos = factor * np.cos(angle)
    deep_sin = factor * np.sin(angle)
    deep = np.concatenate(
        [
            np.concatenate([deep_cos, deep_sin], axis=1),
            np.concatenate([-deep_sin, deep_cos], axis=1),
        ],
        axis=0,
    )
    return wide, deep


def forward_kernel(
    cells_hbm, wide_high_hbm, wide_low_hbm, deep_high_hbm, deep_low_hbm, out_ref,
    cells_ref, wide_high, wide_low, deep_high, deep_low, middle_ref, sems
):
    half = cells_ref.shape[0] // 2
    chunks = [pl.ds(0, half), pl.ds(half, half)]
    moves = [
        (wide_high_hbm, wide_high),
        (wide_low_hbm, wide_low),
        (cells_hbm.at[chunks[0]], cells_ref.at[chunks[0]]),
        (cells_hbm.at[chunks[1]], cells_ref.at[chunks[1]]),
        (deep_high_hbm, deep_high),
        (deep_low_hbm, deep_low),
    ]
    copies = [pltpu.make_async_copy(*pair, sems.at[i]) for i, pair in enumerate(moves)]
    for copy in copies:
        copy.start()
    for copy in copies[:3]:
        copy.wait()
    channels = middle_ref.shape[0] // KY
    block = wide_high.shape[1]
    groups = channels // GROUP
    wide = (wide_high[...], wide_low[...])
    for first in range(0, groups, 2):
        if first == groups // 2:
            copies[3].wait()
        cells = jnp.concatenate(
            [
                cells_ref[first * block : (first + 1) * block, :],
                cells_ref[(first + 1) * block : (first + 2) * block, :],
            ],
            axis=1,
        )
        summed = product_of_halves(wide, halves_of(cells), ((1,), (0,)))
        for part in range(2):
            for mode in range(KY):
                row = (part * KY + mode) * GROUP
                for side in range(2):
                    place = mode * channels + (first + side) * GROUP
                    middle_ref[place : place + GROUP, part * LANES : (part + 1) * LANES] = (
                        summed[row : row + GROUP, side * LANES : (side + 1) * LANES]
                    )
    copies[4].wait()
    copies[5].wait()
    modes = product_of_halves(
        (deep_high[...], deep_low[...]), halves_of(middle_ref[...]), ((1,), (1,))
    )
    for mode in range(KY):
        for part in range(2):
            for odd in range(2):
                lane = odd * 2 * channels + part * channels
                row = (part * 2 + odd) * (KZ // 2)
                out_ref[mode * KZ // 2 : (mode + 1) * KZ // 2, lane : lane + channels] = modes[
                    row : row + KZ // 2, mode * channels : (mode + 1) * channels
                ]


def crossed(value, channels, sign):
    lane = lax.broadcasted_iota(jnp.int32, value.shape, 1)
    width = value.shape[1]
    return jnp.where(
        lane % (2 * channels) < channels,
        sign * pltpu.roll(value, width - channels, axis=1),
        -sign * pltpu.roll(value, channels, axis=1),
    )


def gather_kernel(rows_ref, basis_ref, out_ref, *, channels, share):
    length = basis_ref.shape[1]
    cells = jnp.concatenate(
        [rows_ref[pl.ds(0, length, stride=2), :], rows_ref[pl.ds(1, length, stride=2), :]], axis=1
    )
    sums = jnp.dot(basis_ref[...], cells, precision=highest, preferred_element_type=f32)
    for tile in range(2):
        lanes = slice(tile * LANES, (tile + 1) * LANES)
        modes = sums[:KX, lanes] + crossed(sums[KX:, lanes], channels, 1.0)
        start = 2 * tile * KX
        out_ref[start : start + KX, :] = modes
        out_ref[start + KX : start + 2 * KX, :] = pltpu.roll(modes, LANES // 2, axis=1)


def spread_kernel(rows_ref, basis_ref, out_ref, *, channels):
    length = basis_ref.shape[1]
    for tile in range(2):
        start = 2 * tile * KX
        even = rows_ref[start : start + KX, :]
        odd = pltpu.roll(rows_ref[start + KX : start + 2 * KX, :], LANES // 2, axis=1)
        lane = lax.broadcasted_iota(jnp.int32, even.shape, 1)
        modes = jnp.where(lane < LANES // 2, even, odd)
        both = jnp.concatenate([modes, crossed(modes, channels, -1.0)], axis=0)
        out_ref[pl.ds(tile, length, stride=2), :] = lax.dot_general(
            basis_ref[...],
            both,
            (((0,), (0,)), ((), ())),
            precision=highest,
            preferred_element_type=f32,
        )


def middle_kernel(rows_ref, weight_ref, out_ref, *, channels, norm_factor):
    share = weight_ref.shape[0]
    sums = rows_ref[:share, :]
    for start in range(share, rows_ref.shape[0], share):
        sums = sums + rows_ref[start : start + share, :]
    sums = norm_factor * sums
    hat_real = sums[:, :channels]
    hat_imag = sums[:, channels : 2 * channels]
    size = channels * channels
    lane = lax.broadcasted_iota(jnp.int32, (channels, size), 1)
    row = lax.broadcasted_iota(jnp.int32, (channels, size), 0)
    spread = jnp.where(lane // channels == row, 1.0, 0.0).astype(f32)
    hat = jnp.dot(
        jnp.concatenate([hat_real, hat_imag], axis=0),
        spread,
        precision=highest,
        preferred_element_type=f32,
    )
    real = hat[:share]
    imag = hat[share:]
    weight_real = weight_ref[:, :size]
    weight_imag = weight_ref[:, size:]
    terms = jnp.concatenate(
        [real * weight_real - imag * weight_imag, real * weight_imag + imag * weight_real], axis=0
    )
    mixed = terms[:, :LANES]
    for start in range(LANES, size, LANES):
        mixed = mixed + terms[:, start : start + LANES]
    step = LANES // 2
    while step >= channels:
        mixed = mixed + pltpu.roll(mixed, step, axis=1)
        step = step // 2
    lane = lax.broadcasted_iota(jnp.int32, (share, LANES), 1)
    mixed_real = mixed[:share]
    mixed_imag = mixed[share:]
    mixed = jnp.where(lane < channels, mixed_real, mixed_imag)
    for start in range(0, out_ref.shape[0], share):
        out_ref[start : start + share, :] = mixed


def edges_kernel(left_ref, cells_ref, right_ref, tails_ref, heads_ref, *, rows_y, channels):
    planes = (left_ref, cells_ref, right_ref)
    for plane in range(3):
        rows = pl.ds(plane * channels, channels)
        heads_ref[rows, :] = planes[plane][pl.ds(0, channels, stride=rows_y), :]
        tails_ref[rows, :] = planes[plane][pl.ds(rows_y - 1, channels, stride=rows_y), :]


def doubled_taps(taps):
    high, low = halves_of(taps)
    return jnp.concatenate([high, high, low], axis=1)


def doubled_cells(cells):
    high, low = halves_of(cells)
    return jnp.concatenate([high, low, high], axis=0)


def shifted_sum(parts, depth):
    lane = lax.broadcasted_iota(jnp.int32, parts[1].shape, 1)
    below = jnp.where(lane == 0, 0.0, pltpu.roll(parts[0], 1, axis=1))
    above = jnp.where(lane == depth - 1, 0.0, pltpu.roll(parts[2], depth - 1, axis=1))
    return parts[1] + below + above


def conv_kernel(*refs, planes, rows_y, channels, depth):
    plane_refs = refs[: len(planes)]
    taps_ref, base_ref, out_ref, sums_scratch = refs[len(planes) :]
    width = 3 * channels
    taps = jnp.concatenate(
        [taps_ref[:, plane * channels : (plane + 1) * channels] for plane in planes], axis=1
    )
    taps = doubled_taps(taps)
    sums_scratch[0, :width, :] = jnp.zeros((width, depth), f32)
    sums_scratch[rows_y + 1, 2 * width :, :] = jnp.zeros((width, depth), f32)

    def row_cells(row):
        return jnp.concatenate(
            [plane[pl.ds(row, channels, stride=rows_y), :] for plane in plane_refs], axis=0
        )

    def collect(row):
        parts = []
        for shift in range(3):
            first = shift * channels
            parts.append(
                sums_scratch[row, first : first + channels, :]
                + sums_scratch[row + 1, width + first : width + first + channels, :]
                + sums_scratch[row + 2, 2 * width + first : 2 * width + first + channels, :]
            )
        place = pl.ds(row, channels, stride=rows_y)
        base = base_ref[place, :] if base_ref.shape == out_ref.shape else base_ref[...]
        out_ref[place, :] = shifted_sum(parts, depth) + base

    for step in range(rows_y // 2):
        cells = jnp.concatenate([row_cells(2 * step), row_cells(2 * step + 1)], axis=1)
        sums = product(taps, doubled_cells(cells), ((1,), (0,)))
        sums_scratch[2 * step + 1] = sums[:, :depth]
        sums_scratch[2 * step + 2] = sums[:, depth:]
        if step:
            collect(2 * step - 2)
            collect(2 * step - 1)
    collect(rows_y - 2)
    collect(rows_y - 1)


def inverse_kernel(
    rows_ref, wide_high, wide_low, deep_high, deep_low, conv_ref, before_ref, after_ref, taps_ref,
    out_ref, modes_ref, middle_ref, conv_scratch, *, rows_y
):
    channels = modes_ref.shape[1] // KY
    groups = channels // GROUP
    depth = conv_ref.shape[1]
    width = 3 * channels
    conv_scratch[...] = conv_ref[...]
    taps = jnp.concatenate([taps_ref[:width, :], taps_ref[2 * width :, :]], axis=0)
    cells = jnp.concatenate([before_ref[...], after_ref[...]], axis=1)
    sums = product(doubled_taps(taps), doubled_cells(cells), ((1,), (0,)))
    for row, values in ((0, sums[:width, :depth]), (rows_y - 1, sums[width:, depth:])):
        place = pl.ds(row, channels, stride=rows_y)
        parts = [values[r * channels : (r + 1) * channels] for r in range(3)]
        conv_scratch[place, :] = conv_scratch[place, :] + shifted_sum(parts, depth)
    for mode in range(KY):
        for part in range(2):
            for odd in range(2):
                lane = odd * 2 * channels + part * channels
                row = (part * 2 + odd) * (KZ // 2)
                modes_ref[row : row + KZ // 2, mode * channels : (mode + 1) * channels] = rows_ref[
                    mode * KZ // 2 : (mode + 1) * KZ // 2, lane : lane + channels
                ]
    deep = product_of_halves(
        halves_of(modes_ref[...]), (deep_high[...], deep_low[...]), ((0,), (0,))
    )
    for group in range(groups):
        for part in range(2):
            for mode in range(KY):
                row = (part * KY + mode) * GROUP
                place = mode * channels + group * GROUP
                middle_ref[row : row + GROUP, group * LANES : (group + 1) * LANES] = deep[
                    place : place + GROUP, part * LANES : (part + 1) * LANES
                ]
    wide = (wide_high[...], wide_low[...])
    block = wide_high.shape[0]
    for first in range(0, groups, 2):
        summed = product_of_halves(
            wide,
            halves_of(middle_ref[:, first * LANES : (first + 2) * LANES]),
            ((1,), (0,)),
        )
        for side in range(2):
            start = (first + side) * block
            value = (
                summed[:, side * LANES : (side + 1) * LANES] + conv_scratch[start : start + block, :]
            )
            out_ref[start : start + block, :] = (
                0.5 * value * (1.0 + lax.erf(value * math.sqrt(0.5)))
            )


def local(features, conv_weight, conv_bias, spectral_weight):
    channels, rows_x, rows_y, depth = features.shape
    count_x = lax.axis_size("gx")
    count_y = lax.axis_size("gy")
    length_x = rows_x * count_x
    length_y = rows_y * count_y
    norm_factor = 1.0 / math.sqrt(length_x * length_y * depth)
    pairs = KY * KZ
    devices = count_x * count_y
    halves = devices // pairs
    share = KX // halves
    params = pltpu.CompilerParams(vmem_limit_bytes=48 * 1024 * 1024)
    cells = features.reshape(channels * rows_y, depth)

    wide, deep = forward_tables(rows_y, length_y, depth)
    outgoing = pl.pallas_call(
        forward_kernel,
        out_shape=jax.ShapeDtypeStruct((pairs // 2, LANES), f32),
        in_specs=[pl.BlockSpec(memory_space=pltpu.HBM)] * 5,
        scratch_shapes=[
            pltpu.VMEM(cells.shape, f32),
            pltpu.VMEM(wide.shape, bf16),
            pltpu.VMEM(wide.shape, bf16),
            pltpu.VMEM(deep.shape, bf16),
            pltpu.VMEM(deep.shape, bf16),
            pltpu.VMEM((KY * channels, 2 * depth), f32),
            pltpu.SemaphoreType.DMA((6,)),
        ],
        compiler_params=params,
        name="forward",
    )(*[
        pltpu.with_memory_space_constraint(value, pltpu.HBM)
        for value in (cells, *fixed_halves(wide), *fixed_halves(deep))
    ])
    taps = jnp.transpose(conv_weight, (1, 2, 4, 0, 3)).reshape(9 * channels, 3 * channels)
    bias = jnp.broadcast_to(conv_bias[:, None], (channels, depth))

    def conv(name, planes, *operands):
        return pl.pallas_call(
            lambda *refs: conv_kernel(
                *refs, planes=planes, rows_y=rows_y, channels=channels, depth=depth
            ),
            out_shape=jax.ShapeDtypeStruct(cells.shape, f32),
            scratch_shapes=[pltpu.VMEM((rows_y + 2, 9 * channels, depth), f32)],
            compiler_params=params,
            name=name,
        )(*operands)

    long_modes = jnp.arange(KX, dtype=jnp.int32)
    long_modes = jnp.where(long_modes < KX // 2, long_modes, length_x - KX + long_modes)
    wide_mode = lax.axis_index("gx") * pairs // count_x // KZ
    wide_mode = jnp.where(wide_mode < KY // 2, wide_mode, length_y - KY + wide_mode)
    places = jnp.arange(length_x, dtype=jnp.int32)
    steps = length_y // length_x * (long_modes[:, None] * places[None, :])
    steps = (steps + wide_mode * rows_y * lax.axis_index("gy")) % length_y
    angle = 2.0 * math.pi / length_y * steps.astype(f32)
    basis = jnp.concatenate([jnp.cos(angle), jnp.sin(angle)], axis=0)

    def small(kernel, name, rows, *operands):
        return pl.pallas_call(
            kernel,
            out_shape=jax.ShapeDtypeStruct((rows, LANES), f32),
            compiler_params=params,
            name=name,
        )(*operands)

    arrived = lax.all_to_all(outgoing, "gx", 0, 0, tiled=True)
    later, arrived = lax.optimization_barrier((features, arrived))
    left = lax.ppermute(later, "gx", [(i, i + 1) for i in range(count_x - 1)])
    right = lax.ppermute(later, "gx", [(i + 1, i) for i in range(count_x - 1)])
    left = left.reshape(cells.shape)
    right = right.reshape(cells.shape)
    edge = jax.ShapeDtypeStruct((3 * channels, depth), f32)
    tails, heads = pl.pallas_call(
        lambda *refs: edges_kernel(*refs, rows_y=rows_y, channels=channels),
        out_shape=(edge, edge),
        compiler_params=params,
        name="edges",
    )(left, cells, right)
    before = lax.ppermute(tails, "gy", [(i, i + 1) for i in range(count_y - 1)])
    after = lax.ppermute(heads, "gy", [(i + 1, i) for i in range(count_y - 1)])
    local_term = conv("conv", (0, 1, 2), left, cells, right, taps, bias)

    partial_modes = small(
        lambda *refs: gather_kernel(*refs, channels=channels, share=share),
        "gather", count_y * share, arrived, basis,
    )
    owned = lax.all_to_all(partial_modes, "gy", 0, 0, tiled=True)
    mixed = small(
        lambda *refs: middle_kernel(*refs, channels=channels, norm_factor=norm_factor),
        "middle", count_y * share, owned, spectral_weight,
    )
    shared = lax.all_to_all(mixed, "gy", 0, 0, tiled=True)
    returning = small(
        lambda *refs: spread_kernel(*refs, channels=channels),
        "spread", pairs // 2, shared, basis,
    )
    whole = lax.all_to_all(returning, "gx", 0, 0, tiled=True)

    wide, deep = inverse_tables(rows_y, length_y, depth, norm_factor)
    layer_out = pl.pallas_call(
        lambda *refs: inverse_kernel(*refs, rows_y=rows_y),
        out_shape=jax.ShapeDtypeStruct((channels * rows_y, depth), f32),
        scratch_shapes=[
            pltpu.VMEM((2 * KZ, KY * channels), f32),
            pltpu.VMEM((2 * KY * GROUP, channels // GROUP * LANES), f32),
            pltpu.VMEM((channels * rows_y, depth), f32),
        ],
        compiler_params=params,
        name="inverse",
    )(whole, *fixed_halves(wide), *fixed_halves(deep), local_term, before, after, taps)
    return layer_out.reshape(features.shape)


def solution(mesh):
    return jax.shard_map(
        local,
        mesh=mesh,
        in_specs=(P(None, "gx", "gy", None), P(), P(), P(("gx", "gy"), None)),
        out_specs=P(None, "gx", "gy", None),
        check_vma=False,
    )
```

```python
import math

import jax
import jax.numpy as jnp
import numpy as np
from jax import lax
from jax.experimental import pallas as pl
from jax.experimental.pallas import tpu as pltpu
from jax.sharding import PartitionSpec as P

KX = 16
KY = 16
KZ = 16
GROUP = 8
CLASSES = 4
LANES = 128

f32 = jnp.float32
bf16 = jnp.bfloat16
highest = lax.Precision.HIGHEST


def halves_of(value):
    high = value.astype(bf16)
    return high, (value - high.astype(f32)).astype(bf16)


def fixed_halves(table):
    table = np.asarray(table, np.float32)
    high = table.astype(bf16)
    return jnp.asarray(high), jnp.asarray((table - high.astype(np.float32)).astype(bf16))


def product(left, right, dims):
    return lax.dot_general(left, right, (dims, ((), ())), preferred_element_type=f32)


def product_of_halves(left, right, dims):
    return (
        product(left[0], right[0], dims)
        + product(left[0], right[1], dims)
        + product(left[1], right[0], dims)
    )


def signed_modes(number):
    series = np.arange(number)
    return np.where(series < number // 2, series, series - number)


def deep_angles(depth, step):
    order = np.concatenate([np.arange(start, KZ, step) for start in range(step)])
    return order, 2.0 * np.pi / depth * np.outer(order, np.arange(depth))


def forward_tables(rows_y, length_y, depth):
    angle = 2.0 * np.pi / length_y * np.outer(signed_modes(KY), np.arange(rows_y))
    same = np.eye(GROUP)
    wide = np.einsum("rby,ij->rbijy", np.stack([np.cos(angle), -np.sin(angle)]), same)
    wide = wide.reshape(2 * KY * GROUP, GROUP * rows_y)
    _, angle = deep_angles(depth, CLASSES)
    deep_cos = np.cos(angle)
    deep_sin = np.sin(angle)
    deep = np.concatenate(
        [
            np.concatenate([deep_cos, deep_sin], axis=1),
            np.concatenate([-deep_sin, deep_cos], axis=1),
        ],
        axis=0,
    )
    return wide, deep


def inverse_tables(rows_y, length_y, depth, norm_factor):
    angle = 2.0 * np.pi / length_y * np.outer(np.arange(rows_y), signed_modes(KY))
    same = np.eye(GROUP)
    wide = np.einsum("ryb,ij->iyrbj", np.stack([np.cos(angle), -np.sin(angle)]), same)
    wide = wide.reshape(GROUP * rows_y, 2 * KY * GROUP)
    order, angle = deep_angles(depth, 2)
    factor = norm_factor * np.where(order == 0, 1.0, 2.0)[:, None]
    deep_cos = factor * np.cos(angle)
    deep_sin = factor * np.sin(angle)
    deep = np.concatenate(
        [
            np.concatenate([deep_cos, deep_sin], axis=1),
            np.concatenate([-deep_sin, deep_cos], axis=1),
        ],
        axis=0,
    )
    return wide, deep


def long_tables(length_x, count_y, share):
    modes = signed_modes(KX)
    angle = 2.0 * np.pi / length_x * np.outer(modes, np.arange(length_x))
    halves = [
        np.concatenate([np.cos(angle[i : i + share]), np.sin(angle[i : i + share])])
        for i in range(0, KX, share)
    ]
    turned = [angle + 2.0 * np.pi / count_y * turn for turn in range(count_y)]
    whole = [np.concatenate([np.cos(each), np.sin(each)]) for each in turned]
    return jnp.asarray(np.concatenate(halves), f32), jnp.asarray(np.concatenate(whole), f32)


def turn_tables(count_y, rows):
    wide = 2 * (np.arange(rows) // (KZ // CLASSES))[:, None] + np.arange(LANES) // (LANES // 2)
    angle = 2.0 * np.pi / count_y * (np.arange(count_y)[:, None, None] * wide % count_y)
    angle = angle.reshape(count_y * rows, LANES)
    return jnp.asarray(np.cos(angle), f32), jnp.asarray(np.sin(angle), f32)


def forward_kernel(
    cells_hbm, wide_high_hbm, wide_low_hbm, deep_high_hbm, deep_low_hbm, out_ref,
    cells_ref, wide_high, wide_low, deep_high, deep_low, middle_ref, pair_ref, sems
):
    half = cells_ref.shape[0] // 2
    chunks = [pl.ds(0, half), pl.ds(half, half)]
    moves = [
        (wide_high_hbm, wide_high),
        (wide_low_hbm, wide_low),
        (cells_hbm.at[chunks[0]], cells_ref.at[chunks[0]]),
        (cells_hbm.at[chunks[1]], cells_ref.at[chunks[1]]),
        (deep_high_hbm, deep_high),
        (deep_low_hbm, deep_low),
    ]
    copies = [pltpu.make_async_copy(*pair, sems.at[i]) for i, pair in enumerate(moves)]
    for copy in copies:
        copy.start()
    for copy in copies[:3]:
        copy.wait()
    channels = middle_ref.shape[0] // KY
    block = wide_high.shape[1]
    groups = channels // GROUP
    wide = (wide_high[...], wide_low[...])
    for first in range(0, groups, 2):
        if first == groups // 2:
            copies[3].wait()
        cells = jnp.concatenate(
            [
                cells_ref[first * block : (first + 1) * block, :],
                cells_ref[(first + 1) * block : (first + 2) * block, :],
            ],
            axis=1,
        )
        summed = product_of_halves(wide, halves_of(cells), ((1,), (0,)))
        for part in range(2):
            for mode in range(KY):
                row = (part * KY + mode) * GROUP
                for side in range(2):
                    place = mode * channels + (first + side) * GROUP
                    middle_ref[place : place + GROUP, part * LANES : (part + 1) * LANES] = (
                        summed[row : row + GROUP, side * LANES : (side + 1) * LANES]
                    )
    copies[4].wait()
    copies[5].wait()
    modes = product_of_halves(
        (deep_high[...], deep_low[...]), halves_of(middle_ref[...]), ((1,), (1,))
    )
    size = KZ // CLASSES
    rows = KY // 2 * size
    for mode in range(KY):
        for part in range(2):
            for kind in range(CLASSES):
                lane = mode % 2 * 2 * channels + part * channels
                row = kind * rows + mode // 2 * size
                source = part * KZ + kind * size
                pair_ref[row : row + size, lane : lane + channels] = modes[
                    source : source + size, mode * channels : (mode + 1) * channels
                ]
    copies_of = out_ref.shape[0] // (CLASSES * rows)
    for kind in range(CLASSES):
        for each in range(copies_of):
            start = (kind * copies_of + each) * rows
            out_ref[start : start + rows, :] = pair_ref[kind * rows : (kind + 1) * rows, :]


def crossed(value, channels, sign):
    lane = lax.broadcasted_iota(jnp.int32, value.shape, 1)
    width = value.shape[1]
    return jnp.where(
        lane % (2 * channels) < channels,
        sign * pltpu.roll(value, width - channels, axis=1),
        -sign * pltpu.roll(value, channels, axis=1),
    )


def fold_kernel(rows_ref, cos_ref, sin_ref, out_ref, *, channels):
    rows = out_ref.shape[0] // 2
    total = jnp.zeros((rows, LANES), f32)
    for start in range(0, rows_ref.shape[0], rows):
        place = slice(start, start + rows)
        value = rows_ref[place, :]
        total = total + value * cos_ref[place, :] + crossed(value, channels, 1.0) * sin_ref[place, :]
    other = pltpu.roll(total, LANES // 2, axis=1)
    size = KZ // CLASSES
    for tile in range(rows // size):
        start = tile * size
        out_ref[2 * start : 2 * start + size, :] = total[start : start + size, :]
        out_ref[2 * start + size : 2 * start + 2 * size, :] = other[start : start + size, :]


def spread_kernel(rows_ref, table_ref, out_ref, *, channels, rows_x):
    length = table_ref.shape[1]
    turns = table_ref.shape[0] // (2 * KX)
    wide_mode = lax.axis_index("gx") // rows_x
    turn = lax.rem(wide_mode * lax.axis_index("gy"), turns)
    basis = table_ref[pl.ds(pl.multiple_of(turn * 2 * KX, 2 * KX), 2 * KX), :]
    for tile in range(2):
        start = 2 * tile * KX
        even = rows_ref[start : start + KX, :]
        odd = pltpu.roll(rows_ref[start + KX : start + 2 * KX, :], LANES // 2, axis=1)
        lane = lax.broadcasted_iota(jnp.int32, even.shape, 1)
        modes = jnp.where(lane < LANES // 2, even, odd)
        both = jnp.concatenate([modes, crossed(modes, channels, -1.0)], axis=0)
        out_ref[pl.ds(tile, length, stride=2), :] = lax.dot_general(
            basis,
            both,
            (((0,), (0,)), ((), ())),
            precision=highest,
            preferred_element_type=f32,
        )


def middle_kernel(rows_ref, table_ref, weight_ref, out_ref, *, channels, norm_factor):
    share = weight_ref.shape[0]
    half = lax.rem(lax.axis_index("gy"), KX // share)
    basis = table_ref[pl.ds(pl.multiple_of(half * 2 * share, 2 * share), 2 * share), :]
    sums = jnp.dot(basis, rows_ref[...], precision=highest, preferred_element_type=f32)
    sums = norm_factor * (sums[:share] + crossed(sums[share:], channels, 1.0))
    hat_real = sums[:, :channels]
    hat_imag = sums[:, channels : 2 * channels]
    size = channels * channels
    lane = lax.broadcasted_iota(jnp.int32, (channels, size), 1)
    row = lax.broadcasted_iota(jnp.int32, (channels, size), 0)
    spread = jnp.where(lane // channels == row, 1.0, 0.0).astype(f32)
    hat = jnp.dot(
        jnp.concatenate([hat_real, hat_imag], axis=0),
        spread,
        precision=highest,
        preferred_element_type=f32,
    )
    real = hat[:share]
    imag = hat[share:]
    weight_real = weight_ref[:, :size]
    weight_imag = weight_ref[:, size:]
    terms = jnp.concatenate(
        [real * weight_real - imag * weight_imag, real * weight_imag + imag * weight_real], axis=0
    )
    mixed = terms[:, :LANES]
    for start in range(LANES, size, LANES):
        mixed = mixed + terms[:, start : start + LANES]
    step = LANES // 2
    while step >= channels:
        mixed = mixed + pltpu.roll(mixed, step, axis=1)
        step = step // 2
    lane = lax.broadcasted_iota(jnp.int32, (share, LANES), 1)
    mixed_real = mixed[:share]
    mixed_imag = mixed[share:]
    mixed = jnp.where(lane < channels, mixed_real, mixed_imag)
    for start in range(0, out_ref.shape[0], share):
        out_ref[start : start + share, :] = mixed


def edges_kernel(left_ref, cells_ref, right_ref, tails_ref, heads_ref, *, rows_y, channels):
    planes = (left_ref, cells_ref, right_ref)
    for plane in range(3):
        rows = pl.ds(plane * channels, channels)
        heads_ref[rows, :] = planes[plane][pl.ds(0, channels, stride=rows_y), :]
        tails_ref[rows, :] = planes[plane][pl.ds(rows_y - 1, channels, stride=rows_y), :]


def doubled_taps(taps):
    high, low = halves_of(taps)
    return jnp.concatenate([high, high, low], axis=1)


def doubled_cells(cells):
    high, low = halves_of(cells)
    return jnp.concatenate([high, low, high], axis=0)


def shifted_sum(parts, depth):
    lane = lax.broadcasted_iota(jnp.int32, parts[1].shape, 1)
    below = jnp.where(lane == 0, 0.0, pltpu.roll(parts[0], 1, axis=1))
    above = jnp.where(lane == depth - 1, 0.0, pltpu.roll(parts[2], depth - 1, axis=1))
    return parts[1] + below + above


def conv_kernel(*refs, planes, rows_y, channels, depth):
    plane_refs = refs[: len(planes)]
    taps_ref, base_ref, out_ref, sums_scratch = refs[len(planes) :]
    width = 3 * channels
    taps = jnp.concatenate(
        [taps_ref[:, plane * channels : (plane + 1) * channels] for plane in planes], axis=1
    )
    taps = doubled_taps(taps)
    sums_scratch[0, :width, :] = jnp.zeros((width, depth), f32)
    sums_scratch[rows_y + 1, 2 * width :, :] = jnp.zeros((width, depth), f32)

    def row_cells(row):
        return jnp.concatenate(
            [plane[pl.ds(row, channels, stride=rows_y), :] for plane in plane_refs], axis=0
        )

    def collect(row):
        parts = []
        for shift in range(3):
            first = shift * channels
            parts.append(
                sums_scratch[row, first : first + channels, :]
                + sums_scratch[row + 1, width + first : width + first + channels, :]
                + sums_scratch[row + 2, 2 * width + first : 2 * width + first + channels, :]
            )
        place = pl.ds(row, channels, stride=rows_y)
        base = base_ref[place, :] if base_ref.shape == out_ref.shape else base_ref[...]
        out_ref[place, :] = shifted_sum(parts, depth) + base

    for step in range(rows_y // 2):
        cells = jnp.concatenate([row_cells(2 * step), row_cells(2 * step + 1)], axis=1)
        sums = product(taps, doubled_cells(cells), ((1,), (0,)))
        sums_scratch[2 * step + 1] = sums[:, :depth]
        sums_scratch[2 * step + 2] = sums[:, depth:]
        if step:
            collect(2 * step - 2)
            collect(2 * step - 1)
    collect(rows_y - 2)
    collect(rows_y - 1)


def inverse_kernel(
    rows_ref, wide_high, wide_low, deep_high, deep_low, conv_ref, before_ref, after_ref, taps_ref,
    out_ref, modes_ref, middle_ref, conv_scratch, *, rows_y
):
    channels = modes_ref.shape[1] // KY
    groups = channels // GROUP
    depth = conv_ref.shape[1]
    width = 3 * channels
    conv_scratch[...] = conv_ref[...]
    taps = jnp.concatenate([taps_ref[:width, :], taps_ref[2 * width :, :]], axis=0)
    cells = jnp.concatenate([before_ref[...], after_ref[...]], axis=1)
    sums = product(doubled_taps(taps), doubled_cells(cells), ((1,), (0,)))
    for row, values in ((0, sums[:width, :depth]), (rows_y - 1, sums[width:, depth:])):
        place = pl.ds(row, channels, stride=rows_y)
        parts = [values[r * channels : (r + 1) * channels] for r in range(3)]
        conv_scratch[place, :] = conv_scratch[place, :] + shifted_sum(parts, depth)
    for mode in range(KY):
        for part in range(2):
            for odd in range(2):
                lane = odd * 2 * channels + part * channels
                row = (part * 2 + odd) * (KZ // 2)
                modes_ref[row : row + KZ // 2, mode * channels : (mode + 1) * channels] = rows_ref[
                    mode * KZ // 2 : (mode + 1) * KZ // 2, lane : lane + channels
                ]
    deep = product_of_halves(
        halves_of(modes_ref[...]), (deep_high[...], deep_low[...]), ((0,), (0,))
    )
    for group in range(groups):
        for part in range(2):
            for mode in range(KY):
                row = (part * KY + mode) * GROUP
                place = mode * channels + group * GROUP
                middle_ref[row : row + GROUP, group * LANES : (group + 1) * LANES] = deep[
                    place : place + GROUP, part * LANES : (part + 1) * LANES
                ]
    wide = (wide_high[...], wide_low[...])
    block = wide_high.shape[0]
    for first in range(0, groups, 2):
        summed = product_of_halves(
            wide,
            halves_of(middle_ref[:, first * LANES : (first + 2) * LANES]),
            ((1,), (0,)),
        )
        for side in range(2):
            start = (first + side) * block
            value = (
                summed[:, side * LANES : (side + 1) * LANES] + conv_scratch[start : start + block, :]
            )
            out_ref[start : start + block, :] = (
                0.5 * value * (1.0 + lax.erf(value * math.sqrt(0.5)))
            )


def local(features, conv_weight, conv_bias, spectral_weight):
    channels, rows_x, rows_y, depth = features.shape
    count_x = lax.axis_size("gx")
    count_y = lax.axis_size("gy")
    length_x = rows_x * count_x
    length_y = rows_y * count_y
    norm_factor = 1.0 / math.sqrt(length_x * length_y * depth)
    pairs = KY * KZ
    devices = count_x * count_y
    halves = devices // pairs
    share = KX // halves
    params = pltpu.CompilerParams(vmem_limit_bytes=48 * 1024 * 1024)
    cells = features.reshape(channels * rows_y, depth)

    wide, deep = forward_tables(rows_y, length_y, depth)
    outgoing = pl.pallas_call(
        forward_kernel,
        out_shape=jax.ShapeDtypeStruct((pairs // 2 // CLASSES * count_y, LANES), f32),
        in_specs=[pl.BlockSpec(memory_space=pltpu.HBM)] * 5,
        scratch_shapes=[
            pltpu.VMEM(cells.shape, f32),
            pltpu.VMEM(wide.shape, bf16),
            pltpu.VMEM(wide.shape, bf16),
            pltpu.VMEM(deep.shape, bf16),
            pltpu.VMEM(deep.shape, bf16),
            pltpu.VMEM((KY * channels, 2 * depth), f32),
            pltpu.VMEM((pairs // 2, LANES), f32),
            pltpu.SemaphoreType.DMA((6,)),
        ],
        compiler_params=params,
        name="forward",
    )(*[
        pltpu.with_memory_space_constraint(value, pltpu.HBM)
        for value in (cells, *fixed_halves(wide), *fixed_halves(deep))
    ])
    taps = jnp.transpose(conv_weight, (1, 2, 4, 0, 3)).reshape(9 * channels, 3 * channels)
    bias = jnp.broadcast_to(conv_bias[:, None], (channels, depth))

    def conv(name, planes, *operands):
        return pl.pallas_call(
            lambda *refs: conv_kernel(
                *refs, planes=planes, rows_y=rows_y, channels=channels, depth=depth
            ),
            out_shape=jax.ShapeDtypeStruct(cells.shape, f32),
            scratch_shapes=[pltpu.VMEM((rows_y + 2, 9 * channels, depth), f32)],
            compiler_params=params,
            name=name,
        )(*operands)

    def small(kernel, name, rows, *operands):
        return pl.pallas_call(
            kernel,
            out_shape=jax.ShapeDtypeStruct((rows, LANES), f32),
            compiler_params=params,
            name=name,
        )(*operands)

    left = lax.ppermute(features, "gx", [(i, i + 1) for i in range(count_x - 1)])
    right = lax.ppermute(features, "gx", [(i + 1, i) for i in range(count_x - 1)])
    left = left.reshape(cells.shape)
    right = right.reshape(cells.shape)
    edge = jax.ShapeDtypeStruct((3 * channels, depth), f32)
    tails, heads = pl.pallas_call(
        lambda *refs: edges_kernel(*refs, rows_y=rows_y, channels=channels),
        out_shape=(edge, edge),
        compiler_params=params,
        name="edges",
    )(left, cells, right)
    before = lax.ppermute(tails, "gy", [(i, i + 1) for i in range(count_y - 1)])
    after = lax.ppermute(heads, "gy", [(i + 1, i) for i in range(count_y - 1)])
    local_term = conv("conv", (0, 1, 2), left, cells, right, taps, bias)

    half_table, whole_table = long_tables(length_x, count_y, share)
    gathered = lax.all_to_all(outgoing, "gy", 0, 0, tiled=True)
    folded = small(
        lambda *refs: fold_kernel(*refs, channels=channels),
        "fold", count_x, gathered, *turn_tables(count_y, count_x // 2),
    )
    arrived = lax.all_to_all(folded, "gx", 0, 0, tiled=True)
    mixed = small(
        lambda *refs: middle_kernel(*refs, channels=channels, norm_factor=norm_factor),
        "middle", count_y * share, arrived, half_table, spectral_weight,
    )
    shared = lax.all_to_all(mixed, "gy", 0, 0, tiled=True)
    returning = small(
        lambda *refs: spread_kernel(*refs, channels=channels, rows_x=count_x // KY),
        "spread", pairs // 2, shared, whole_table,
    )
    whole = lax.all_to_all(returning, "gx", 0, 0, tiled=True)

    wide, deep = inverse_tables(rows_y, length_y, depth, norm_factor)
    layer_out = pl.pallas_call(
        lambda *refs: inverse_kernel(*refs, rows_y=rows_y),
        out_shape=jax.ShapeDtypeStruct((channels * rows_y, depth), f32),
        scratch_shapes=[
            pltpu.VMEM((2 * KZ, KY * channels), f32),
            pltpu.VMEM((2 * KY * GROUP, channels // GROUP * LANES), f32),
            pltpu.VMEM((channels * rows_y, depth), f32),
        ],
        compiler_params=params,
        name="inverse",
    )(whole, *fixed_halves(wide), *fixed_halves(deep), local_term, before, after, taps)
    return layer_out.reshape(features.shape)


def solution(mesh):
    return jax.shard_map(
        local,
        mesh=mesh,
        in_specs=(P(None, "gx", "gy", None), P(), P(), P(("gx", "gy"), None)),
        out_specs=P(None, "gx", "gy", None),
        check_vma=False,
    )
```

```python
import math

import jax
import jax.numpy as jnp
import numpy as np
from jax import lax
from jax.experimental import pallas as pl
from jax.experimental.pallas import tpu as pltpu
from jax.sharding import PartitionSpec as P

KX = 16
KY = 16
KZ = 16
GROUP = 8
CLASSES = 4
LANES = 128
LONG = pl.CostEstimate(flops=10**10, transcendentals=0, bytes_accessed=1 << 20)
COSTLY = dict.fromkeys(("middle",), LONG)

f32 = jnp.float32
bf16 = jnp.bfloat16
highest = lax.Precision.HIGHEST


def halves_of(value):
    high = value.astype(bf16)
    return high, (value - high.astype(f32)).astype(bf16)


def fixed_halves(table):
    table = np.asarray(table, np.float32)
    high = table.astype(bf16)
    return jnp.asarray(high), jnp.asarray((table - high.astype(np.float32)).astype(bf16))


def product(left, right, dims):
    return lax.dot_general(left, right, (dims, ((), ())), preferred_element_type=f32)


def product_of_halves(left, right, dims):
    return (
        product(left[0], right[0], dims)
        + product(left[0], right[1], dims)
        + product(left[1], right[0], dims)
    )


def signed_modes(number):
    series = np.arange(number)
    return np.where(series < number // 2, series, series - number)


def deep_angles(depth, step):
    order = np.concatenate([np.arange(start, KZ, step) for start in range(step)])
    return order, 2.0 * np.pi / depth * np.outer(order, np.arange(depth))


def forward_tables(rows_y, length_y, depth):
    angle = 2.0 * np.pi / length_y * np.outer(signed_modes(KY), np.arange(rows_y))
    same = np.eye(GROUP)
    wide = np.einsum("rby,ij->rbijy", np.stack([np.cos(angle), -np.sin(angle)]), same)
    wide = wide.reshape(2 * KY * GROUP, GROUP * rows_y)
    _, angle = deep_angles(depth, CLASSES)
    deep_cos = np.cos(angle)
    deep_sin = np.sin(angle)
    deep = np.concatenate(
        [
            np.concatenate([deep_cos, deep_sin], axis=1),
            np.concatenate([-deep_sin, deep_cos], axis=1),
        ],
        axis=0,
    )
    return wide, deep


def inverse_tables(rows_y, length_y, depth, norm_factor):
    angle = 2.0 * np.pi / length_y * np.outer(np.arange(rows_y), signed_modes(KY))
    same = np.eye(GROUP)
    wide = np.einsum("ryb,ij->iyrbj", np.stack([np.cos(angle), -np.sin(angle)]), same)
    wide = wide.reshape(GROUP * rows_y, 2 * KY * GROUP)
    order, angle = deep_angles(depth, 2)
    factor = norm_factor * np.where(order == 0, 1.0, 2.0)[:, None]
    deep_cos = factor * np.cos(angle)
    deep_sin = factor * np.sin(angle)
    deep = np.concatenate(
        [
            np.concatenate([deep_cos, deep_sin], axis=1),
            np.concatenate([-deep_sin, deep_cos], axis=1),
        ],
        axis=0,
    )
    return wide, deep


def long_tables(length_x, count_y, share):
    modes = signed_modes(KX)
    angle = 2.0 * np.pi / length_x * np.outer(modes, np.arange(length_x))
    halves = [
        np.concatenate([np.cos(angle[i : i + share]), np.sin(angle[i : i + share])])
        for i in range(0, KX, share)
    ]
    turned = [angle + 2.0 * np.pi / count_y * turn for turn in range(count_y)]
    whole = [np.concatenate([np.cos(each), np.sin(each)]) for each in turned]
    return jnp.asarray(np.concatenate(halves), f32), jnp.asarray(np.concatenate(whole), f32)


def turn_tables(count_y, rows):
    wide = 2 * (np.arange(rows) // (KZ // CLASSES))[:, None] + np.arange(LANES) // (LANES // 2)
    angle = 2.0 * np.pi / count_y * (np.arange(count_y)[:, None, None] * wide % count_y)
    angle = angle.reshape(count_y * rows, LANES)
    return jnp.asarray(np.cos(angle), f32), jnp.asarray(np.sin(angle), f32)


def forward_kernel(
    cells_hbm, wide_high_hbm, wide_low_hbm, deep_high_hbm, deep_low_hbm, out_ref,
    cells_ref, wide_high, wide_low, deep_high, deep_low, middle_ref, pair_ref, sems
):
    half = cells_ref.shape[0] // 2
    chunks = [pl.ds(0, half), pl.ds(half, half)]
    moves = [
        (wide_high_hbm, wide_high),
        (wide_low_hbm, wide_low),
        (cells_hbm.at[chunks[0]], cells_ref.at[chunks[0]]),
        (cells_hbm.at[chunks[1]], cells_ref.at[chunks[1]]),
        (deep_high_hbm, deep_high),
        (deep_low_hbm, deep_low),
    ]
    copies = [pltpu.make_async_copy(*pair, sems.at[i]) for i, pair in enumerate(moves)]
    for copy in copies:
        copy.start()
    for copy in copies[:3]:
        copy.wait()
    channels = middle_ref.shape[0] // KY
    block = wide_high.shape[1]
    groups = channels // GROUP
    wide = (wide_high[...], wide_low[...])
    for first in range(0, groups, 2):
        if first == groups // 2:
            copies[3].wait()
        cells = jnp.concatenate(
            [
                cells_ref[first * block : (first + 1) * block, :],
                cells_ref[(first + 1) * block : (first + 2) * block, :],
            ],
            axis=1,
        )
        summed = product_of_halves(wide, halves_of(cells), ((1,), (0,)))
        for part in range(2):
            for mode in range(KY):
                row = (part * KY + mode) * GROUP
                for side in range(2):
                    place = mode * channels + (first + side) * GROUP
                    middle_ref[place : place + GROUP, part * LANES : (part + 1) * LANES] = (
                        summed[row : row + GROUP, side * LANES : (side + 1) * LANES]
                    )
    copies[4].wait()
    copies[5].wait()
    modes = product_of_halves(
        (deep_high[...], deep_low[...]), halves_of(middle_ref[...]), ((1,), (1,))
    )
    size = KZ // CLASSES
    rows = KY // 2 * size
    for mode in range(KY):
        for part in range(2):
            for kind in range(CLASSES):
                lane = mode % 2 * 2 * channels + part * channels
                row = kind * rows + mode // 2 * size
                source = part * KZ + kind * size
                pair_ref[row : row + size, lane : lane + channels] = modes[
                    source : source + size, mode * channels : (mode + 1) * channels
                ]
    copies_of = out_ref.shape[0] // (CLASSES * rows)
    for kind in range(CLASSES):
        for each in range(copies_of):
            start = (kind * copies_of + each) * rows
            out_ref[start : start + rows, :] = pair_ref[kind * rows : (kind + 1) * rows, :]


def crossed(value, channels, sign):
    lane = lax.broadcasted_iota(jnp.int32, value.shape, 1)
    width = value.shape[1]
    return jnp.where(
        lane % (2 * channels) < channels,
        sign * pltpu.roll(value, width - channels, axis=1),
        -sign * pltpu.roll(value, channels, axis=1),
    )


def fold_kernel(rows_ref, cos_ref, sin_ref, out_ref, *, channels):
    rows = out_ref.shape[0] // 2
    total = jnp.zeros((rows, LANES), f32)
    for start in range(0, rows_ref.shape[0], rows):
        place = slice(start, start + rows)
        value = rows_ref[place, :]
        total = total + value * cos_ref[place, :] + crossed(value, channels, 1.0) * sin_ref[place, :]
    other = pltpu.roll(total, LANES // 2, axis=1)
    size = KZ // CLASSES
    for tile in range(rows // size):
        start = tile * size
        out_ref[2 * start : 2 * start + size, :] = total[start : start + size, :]
        out_ref[2 * start + size : 2 * start + 2 * size, :] = other[start : start + size, :]


def spread_kernel(rows_ref, table_ref, out_ref, *, channels, rows_x):
    length = table_ref.shape[1]
    turns = table_ref.shape[0] // (2 * KX)
    wide_mode = lax.axis_index("gx") // rows_x
    turn = lax.rem(wide_mode * lax.axis_index("gy"), turns)
    basis = table_ref[pl.ds(pl.multiple_of(turn * 2 * KX, 2 * KX), 2 * KX), :]
    for tile in range(2):
        start = 2 * tile * KX
        even = rows_ref[start : start + KX, :]
        odd = pltpu.roll(rows_ref[start + KX : start + 2 * KX, :], LANES // 2, axis=1)
        lane = lax.broadcasted_iota(jnp.int32, even.shape, 1)
        modes = jnp.where(lane < LANES // 2, even, odd)
        both = jnp.concatenate([modes, crossed(modes, channels, -1.0)], axis=0)
        out_ref[pl.ds(tile, length, stride=2), :] = lax.dot_general(
            basis,
            both,
            (((0,), (0,)), ((), ())),
            precision=highest,
            preferred_element_type=f32,
        )


def middle_kernel(rows_ref, table_ref, weight_ref, out_ref, *, channels, norm_factor):
    share = weight_ref.shape[0]
    half = lax.rem(lax.axis_index("gy"), KX // share)
    basis = table_ref[pl.ds(pl.multiple_of(half * 2 * share, 2 * share), 2 * share), :]
    sums = jnp.dot(basis, rows_ref[...], precision=highest, preferred_element_type=f32)
    sums = norm_factor * (sums[:share] + crossed(sums[share:], channels, 1.0))
    hat_real = sums[:, :channels]
    hat_imag = sums[:, channels : 2 * channels]
    size = channels * channels
    lane = lax.broadcasted_iota(jnp.int32, (channels, size), 1)
    row = lax.broadcasted_iota(jnp.int32, (channels, size), 0)
    spread = jnp.where(lane // channels == row, 1.0, 0.0).astype(f32)
    hat = jnp.dot(
        jnp.concatenate([hat_real, hat_imag], axis=0),
        spread,
        precision=highest,
        preferred_element_type=f32,
    )
    real = hat[:share]
    imag = hat[share:]
    weight_real = weight_ref[:, :size]
    weight_imag = weight_ref[:, size:]
    terms = jnp.concatenate(
        [real * weight_real - imag * weight_imag, real * weight_imag + imag * weight_real], axis=0
    )
    mixed = terms[:, :LANES]
    for start in range(LANES, size, LANES):
        mixed = mixed + terms[:, start : start + LANES]
    step = LANES // 2
    while step >= channels:
        mixed = mixed + pltpu.roll(mixed, step, axis=1)
        step = step // 2
    lane = lax.broadcasted_iota(jnp.int32, (share, LANES), 1)
    mixed_real = mixed[:share]
    mixed_imag = mixed[share:]
    mixed = jnp.where(lane < channels, mixed_real, mixed_imag)
    for start in range(0, out_ref.shape[0], share):
        out_ref[start : start + share, :] = mixed


def edges_kernel(left_ref, cells_ref, right_ref, tails_ref, heads_ref, *, rows_y, channels):
    planes = (left_ref, cells_ref, right_ref)
    for plane in range(3):
        rows = pl.ds(plane * channels, channels)
        heads_ref[rows, :] = planes[plane][pl.ds(0, channels, stride=rows_y), :]
        tails_ref[rows, :] = planes[plane][pl.ds(rows_y - 1, channels, stride=rows_y), :]


def doubled_taps(taps):
    high, low = halves_of(taps)
    return jnp.concatenate([high, high, low], axis=1)


def doubled_cells(cells):
    high, low = halves_of(cells)
    return jnp.concatenate([high, low, high], axis=0)


def shifted_sum(parts, depth):
    lane = lax.broadcasted_iota(jnp.int32, parts[1].shape, 1)
    below = jnp.where(lane == 0, 0.0, pltpu.roll(parts[0], 1, axis=1))
    above = jnp.where(lane == depth - 1, 0.0, pltpu.roll(parts[2], depth - 1, axis=1))
    return parts[1] + below + above


def conv_kernel(*refs, planes, rows_y, channels, depth):
    plane_refs = refs[: len(planes)]
    taps_ref, base_ref, out_ref, sums_scratch = refs[len(planes) :]
    width = 3 * channels
    taps = jnp.concatenate(
        [taps_ref[:, plane * channels : (plane + 1) * channels] for plane in planes], axis=1
    )
    taps = doubled_taps(taps)
    sums_scratch[0, :width, :] = jnp.zeros((width, depth), f32)
    sums_scratch[rows_y + 1, 2 * width :, :] = jnp.zeros((width, depth), f32)

    def row_cells(row):
        return jnp.concatenate(
            [plane[pl.ds(row, channels, stride=rows_y), :] for plane in plane_refs], axis=0
        )

    def collect(row):
        parts = []
        for shift in range(3):
            first = shift * channels
            parts.append(
                sums_scratch[row, first : first + channels, :]
                + sums_scratch[row + 1, width + first : width + first + channels, :]
                + sums_scratch[row + 2, 2 * width + first : 2 * width + first + channels, :]
            )
        place = pl.ds(row, channels, stride=rows_y)
        base = base_ref[place, :] if base_ref.shape == out_ref.shape else base_ref[...]
        out_ref[place, :] = shifted_sum(parts, depth) + base

    for step in range(rows_y // 2):
        cells = jnp.concatenate([row_cells(2 * step), row_cells(2 * step + 1)], axis=1)
        sums = product(taps, doubled_cells(cells), ((1,), (0,)))
        sums_scratch[2 * step + 1] = sums[:, :depth]
        sums_scratch[2 * step + 2] = sums[:, depth:]
        if step:
            collect(2 * step - 2)
            collect(2 * step - 1)
    collect(rows_y - 2)
    collect(rows_y - 1)


def inverse_kernel(
    rows_ref, wide_high, wide_low, deep_high, deep_low, conv_ref, before_ref, after_ref, taps_ref,
    out_ref, modes_ref, middle_ref, conv_scratch, *, rows_y
):
    channels = modes_ref.shape[1] // KY
    groups = channels // GROUP
    depth = conv_ref.shape[1]
    width = 3 * channels
    conv_scratch[...] = conv_ref[...]
    taps = jnp.concatenate([taps_ref[:width, :], taps_ref[2 * width :, :]], axis=0)
    cells = jnp.concatenate([before_ref[...], after_ref[...]], axis=1)
    sums = product(doubled_taps(taps), doubled_cells(cells), ((1,), (0,)))
    for row, values in ((0, sums[:width, :depth]), (rows_y - 1, sums[width:, depth:])):
        place = pl.ds(row, channels, stride=rows_y)
        parts = [values[r * channels : (r + 1) * channels] for r in range(3)]
        conv_scratch[place, :] = conv_scratch[place, :] + shifted_sum(parts, depth)
    for mode in range(KY):
        for part in range(2):
            for odd in range(2):
                lane = odd * 2 * channels + part * channels
                row = (part * 2 + odd) * (KZ // 2)
                modes_ref[row : row + KZ // 2, mode * channels : (mode + 1) * channels] = rows_ref[
                    mode * KZ // 2 : (mode + 1) * KZ // 2, lane : lane + channels
                ]
    deep = product_of_halves(
        halves_of(modes_ref[...]), (deep_high[...], deep_low[...]), ((0,), (0,))
    )
    for group in range(groups):
        for part in range(2):
            for mode in range(KY):
                row = (part * KY + mode) * GROUP
                place = mode * channels + group * GROUP
                middle_ref[row : row + GROUP, group * LANES : (group + 1) * LANES] = deep[
                    place : place + GROUP, part * LANES : (part + 1) * LANES
                ]
    wide = (wide_high[...], wide_low[...])
    block = wide_high.shape[0]
    for first in range(0, groups, 2):
        summed = product_of_halves(
            wide,
            halves_of(middle_ref[:, first * LANES : (first + 2) * LANES]),
            ((1,), (0,)),
        )
        for side in range(2):
            start = (first + side) * block
            value = (
                summed[:, side * LANES : (side + 1) * LANES] + conv_scratch[start : start + block, :]
            )
            out_ref[start : start + block, :] = (
                0.5 * value * (1.0 + lax.erf(value * math.sqrt(0.5)))
            )


def local(features, conv_weight, conv_bias, spectral_weight):
    channels, rows_x, rows_y, depth = features.shape
    count_x = lax.axis_size("gx")
    count_y = lax.axis_size("gy")
    length_x = rows_x * count_x
    length_y = rows_y * count_y
    norm_factor = 1.0 / math.sqrt(length_x * length_y * depth)
    pairs = KY * KZ
    devices = count_x * count_y
    halves = devices // pairs
    share = KX // halves
    params = pltpu.CompilerParams(vmem_limit_bytes=48 * 1024 * 1024)
    cells = features.reshape(channels * rows_y, depth)

    wide, deep = forward_tables(rows_y, length_y, depth)
    outgoing = pl.pallas_call(
        forward_kernel,
        out_shape=jax.ShapeDtypeStruct((pairs // 2 // CLASSES * count_y, LANES), f32),
        in_specs=[pl.BlockSpec(memory_space=pltpu.HBM)] * 5,
        scratch_shapes=[
            pltpu.VMEM(cells.shape, f32),
            pltpu.VMEM(wide.shape, bf16),
            pltpu.VMEM(wide.shape, bf16),
            pltpu.VMEM(deep.shape, bf16),
            pltpu.VMEM(deep.shape, bf16),
            pltpu.VMEM((KY * channels, 2 * depth), f32),
            pltpu.VMEM((pairs // 2, LANES), f32),
            pltpu.SemaphoreType.DMA((6,)),
        ],
        compiler_params=params,
        name="forward",
    )(*[
        pltpu.with_memory_space_constraint(value, pltpu.HBM)
        for value in (cells, *fixed_halves(wide), *fixed_halves(deep))
    ])
    taps = jnp.transpose(conv_weight, (1, 2, 4, 0, 3)).reshape(9 * channels, 3 * channels)
    bias = jnp.broadcast_to(conv_bias[:, None], (channels, depth))

    def conv(name, planes, *operands):
        return pl.pallas_call(
            lambda *refs: conv_kernel(
                *refs, planes=planes, rows_y=rows_y, channels=channels, depth=depth
            ),
            out_shape=jax.ShapeDtypeStruct(cells.shape, f32),
            scratch_shapes=[pltpu.VMEM((rows_y + 2, 9 * channels, depth), f32)],
            compiler_params=params,
            cost_estimate=COSTLY.get(name),
            name=name,
        )(*operands)

    def small(kernel, name, rows, *operands):
        return pl.pallas_call(
            kernel,
            out_shape=jax.ShapeDtypeStruct((rows, LANES), f32),
            compiler_params=params,
            cost_estimate=COSTLY.get(name),
            name=name,
        )(*operands)

    right = lax.ppermute(features, "gx", [(i + 1, i) for i in range(count_x - 1)])
    left = lax.ppermute(features, "gx", [(i, i + 1) for i in range(count_x - 1)])
    half_table, whole_table = long_tables(length_x, count_y, share)
    gathered = lax.all_to_all(outgoing, "gy", 0, 0, tiled=True)
    folded = small(
        lambda *refs: fold_kernel(*refs, channels=channels),
        "fold", count_x, gathered, *turn_tables(count_y, count_x // 2),
    )
    arrived = lax.all_to_all(folded, "gx", 0, 0, tiled=True)
    mixed = small(
        lambda *refs: middle_kernel(*refs, channels=channels, norm_factor=norm_factor),
        "middle", count_y * share, arrived, half_table, spectral_weight,
    )
    left = left.reshape(cells.shape)
    right = right.reshape(cells.shape)
    edge = jax.ShapeDtypeStruct((3 * channels, depth), f32)
    tails, heads = pl.pallas_call(
        lambda *refs: edges_kernel(*refs, rows_y=rows_y, channels=channels),
        out_shape=(edge, edge),
        compiler_params=params,
        name="edges",
    )(left, cells, right)
    before = lax.ppermute(tails, "gy", [(i, i + 1) for i in range(count_y - 1)])
    after = lax.ppermute(heads, "gy", [(i + 1, i) for i in range(count_y - 1)])
    local_term = conv("conv", (0, 1, 2), left, cells, right, taps, bias)

    shared = lax.all_to_all(mixed, "gy", 0, 0, tiled=True)
    returning = small(
        lambda *refs: spread_kernel(*refs, channels=channels, rows_x=count_x // KY),
        "spread", pairs // 2, shared, whole_table,
    )
    whole = lax.all_to_all(returning, "gx", 0, 0, tiled=True)

    wide, deep = inverse_tables(rows_y, length_y, depth, norm_factor)
    layer_out = pl.pallas_call(
        lambda *refs: inverse_kernel(*refs, rows_y=rows_y),
        out_shape=jax.ShapeDtypeStruct((channels * rows_y, depth), f32),
        scratch_shapes=[
            pltpu.VMEM((2 * KZ, KY * channels), f32),
            pltpu.VMEM((2 * KY * GROUP, channels // GROUP * LANES), f32),
            pltpu.VMEM((channels * rows_y, depth), f32),
        ],
        compiler_params=params,
        name="inverse",
    )(whole, *fixed_halves(wide), *fixed_halves(deep), local_term, before, after, taps)
    return layer_out.reshape(features.shape)


def solution(mesh):
    return jax.shard_map(
        local,
        mesh=mesh,
        in_specs=(P(None, "gx", "gy", None), P(), P(), P(("gx", "gy"), None)),
        out_specs=P(None, "gx", "gy", None),
        check_vma=False,
    )
```

```python
import math

import jax
import jax.numpy as jnp
import numpy as np
from jax import lax
from jax.experimental import pallas as pl
from jax.experimental.pallas import tpu as pltpu
from jax.sharding import PartitionSpec as P

KX = 16
KY = 16
KZ = 16
GROUP = 8
CLASSES = 4
LANES = 128
LONG = pl.CostEstimate(flops=10**10, transcendentals=0, bytes_accessed=1 << 20)
COSTLY = dict.fromkeys(("middle",), LONG)

f32 = jnp.float32
bf16 = jnp.bfloat16
highest = lax.Precision.HIGHEST


def halves_of(value):
    high = value.astype(bf16)
    return high, (value - high.astype(f32)).astype(bf16)


def fixed_halves(table):
    table = np.asarray(table, np.float32)
    high = table.astype(bf16)
    return jnp.asarray(high), jnp.asarray((table - high.astype(np.float32)).astype(bf16))


def product(left, right, dims):
    return lax.dot_general(left, right, (dims, ((), ())), preferred_element_type=f32)


def product_of_halves(left, right, dims):
    return (
        product(left[0], right[0], dims)
        + product(left[0], right[1], dims)
        + product(left[1], right[0], dims)
    )


def signed_modes(number):
    series = np.arange(number)
    return np.where(series < number // 2, series, series - number)


def deep_angles(depth, step):
    order = np.concatenate([np.arange(start, KZ, step) for start in range(step)])
    return order, 2.0 * np.pi / depth * np.outer(order, np.arange(depth))


def forward_tables(rows_y, length_y, depth):
    angle = 2.0 * np.pi / length_y * np.outer(signed_modes(KY), np.arange(rows_y))
    same = np.eye(GROUP)
    wide = np.einsum("rby,ij->rbijy", np.stack([np.cos(angle), -np.sin(angle)]), same)
    wide = wide.reshape(2 * KY * GROUP, GROUP * rows_y)
    _, angle = deep_angles(depth, CLASSES)
    deep_cos = np.cos(angle)
    deep_sin = np.sin(angle)
    deep = np.concatenate(
        [
            np.concatenate([deep_cos, deep_sin], axis=1),
            np.concatenate([-deep_sin, deep_cos], axis=1),
        ],
        axis=0,
    )
    return wide, deep


def inverse_tables(rows_y, length_y, depth, norm_factor):
    angle = 2.0 * np.pi / length_y * np.outer(np.arange(rows_y), signed_modes(KY))
    same = np.eye(GROUP)
    wide = np.einsum("ryb,ij->iyrbj", np.stack([np.cos(angle), -np.sin(angle)]), same)
    wide = wide.reshape(GROUP * rows_y, 2 * KY * GROUP)
    order, angle = deep_angles(depth, 2)
    factor = norm_factor * np.where(order == 0, 1.0, 2.0)[:, None]
    deep_cos = factor * np.cos(angle)
    deep_sin = factor * np.sin(angle)
    deep = np.concatenate(
        [
            np.concatenate([deep_cos, deep_sin], axis=1),
            np.concatenate([-deep_sin, deep_cos], axis=1),
        ],
        axis=0,
    )
    return wide, deep


def long_tables(length_x, count_y, share):
    modes = signed_modes(KX)
    angle = 2.0 * np.pi / length_x * np.outer(modes, np.arange(length_x))
    halves = [
        np.concatenate([np.cos(angle[i : i + share]), np.sin(angle[i : i + share])])
        for i in range(0, KX, share)
    ]
    turned = [angle + 2.0 * np.pi / count_y * turn for turn in range(count_y)]
    whole = [np.concatenate([np.cos(each), np.sin(each)]) for each in turned]
    return jnp.asarray(np.concatenate(halves), f32), jnp.asarray(np.concatenate(whole), f32)


def turn_tables(count_y, rows):
    wide = 2 * (np.arange(rows) // (KZ // CLASSES))[:, None] + np.arange(LANES) // (LANES // 2)
    angle = 2.0 * np.pi / count_y * (np.arange(count_y)[:, None, None] * wide % count_y)
    angle = angle.reshape(count_y * rows, LANES)
    return jnp.asarray(np.cos(angle), f32), jnp.asarray(np.sin(angle), f32)


def forward_kernel(
    cells_hbm, wide_high_hbm, wide_low_hbm, deep_high_hbm, deep_low_hbm, out_ref,
    cells_ref, wide_high, wide_low, deep_high, deep_low, middle_ref, pair_ref, sems
):
    half = cells_ref.shape[0] // 2
    chunks = [pl.ds(0, half), pl.ds(half, half)]
    moves = [
        (wide_high_hbm, wide_high),
        (wide_low_hbm, wide_low),
        (cells_hbm.at[chunks[0]], cells_ref.at[chunks[0]]),
        (cells_hbm.at[chunks[1]], cells_ref.at[chunks[1]]),
        (deep_high_hbm, deep_high),
        (deep_low_hbm, deep_low),
    ]
    copies = [pltpu.make_async_copy(*pair, sems.at[i]) for i, pair in enumerate(moves)]
    for copy in copies:
        copy.start()
    for copy in copies[:3]:
        copy.wait()
    channels = middle_ref.shape[0] // KY
    block = wide_high.shape[1]
    groups = channels // GROUP
    wide = (wide_high[...], wide_low[...])
    for first in range(0, groups, 2):
        if first == groups // 2:
            copies[3].wait()
        cells = jnp.concatenate(
            [
                cells_ref[first * block : (first + 1) * block, :],
                cells_ref[(first + 1) * block : (first + 2) * block, :],
            ],
            axis=1,
        )
        summed = product_of_halves(wide, halves_of(cells), ((1,), (0,)))
        for part in range(2):
            for mode in range(KY):
                row = (part * KY + mode) * GROUP
                for side in range(2):
                    place = mode * channels + (first + side) * GROUP
                    middle_ref[place : place + GROUP, part * LANES : (part + 1) * LANES] = (
                        summed[row : row + GROUP, side * LANES : (side + 1) * LANES]
                    )
    copies[4].wait()
    copies[5].wait()
    modes = product_of_halves(
        (deep_high[...], deep_low[...]), halves_of(middle_ref[...]), ((1,), (1,))
    )
    size = KZ // CLASSES
    rows = KY // 2 * size
    for mode in range(KY):
        for part in range(2):
            for kind in range(CLASSES):
                lane = mode % 2 * 2 * channels + part * channels
                row = kind * rows + mode // 2 * size
                source = part * KZ + kind * size
                pair_ref[row : row + size, lane : lane + channels] = modes[
                    source : source + size, mode * channels : (mode + 1) * channels
                ]
    copies_of = out_ref.shape[0] // (CLASSES * (rows + channels))
    place = lax.axis_index("gy")
    rows_y = cells_ref.shape[0] // channels
    head = cells_ref[pl.ds(0, channels, stride=rows_y), :]
    tail = cells_ref[pl.ds(rows_y - 1, channels, stride=rows_y), :]
    for kind in range(CLASSES):
        for each in range(copies_of):
            owner = kind * copies_of + each
            start = owner * (rows + channels)
            out_ref[start : start + rows, :] = pair_ref[kind * rows : (kind + 1) * rows, :]
            out_ref[start + rows : start + rows + channels, :] = jnp.where(
                place + 1 == owner, tail, head
            )


def crossed(value, channels, sign):
    lane = lax.broadcasted_iota(jnp.int32, value.shape, 1)
    width = value.shape[1]
    return jnp.where(
        lane % (2 * channels) < channels,
        sign * pltpu.roll(value, width - channels, axis=1),
        -sign * pltpu.roll(value, channels, axis=1),
    )


def fold_kernel(rows_ref, cos_ref, sin_ref, out_ref, *, channels):
    rows = out_ref.shape[0] // 2
    total = jnp.zeros((rows, LANES), f32)
    for start in range(0, cos_ref.shape[0], rows):
        place = slice(start, start + rows)
        source = start // rows * (rows + channels)
        value = rows_ref[source : source + rows, :]
        total = total + value * cos_ref[place, :] + crossed(value, channels, 1.0) * sin_ref[place, :]
    other = pltpu.roll(total, LANES // 2, axis=1)
    size = KZ // CLASSES
    for tile in range(rows // size):
        start = tile * size
        out_ref[2 * start : 2 * start + size, :] = total[start : start + size, :]
        out_ref[2 * start + size : 2 * start + 2 * size, :] = other[start : start + size, :]


def spread_kernel(rows_ref, table_ref, out_ref, *, channels, rows_x):
    length = table_ref.shape[1]
    turns = table_ref.shape[0] // (2 * KX)
    wide_mode = lax.axis_index("gx") // rows_x
    turn = lax.rem(wide_mode * lax.axis_index("gy"), turns)
    basis = table_ref[pl.ds(pl.multiple_of(turn * 2 * KX, 2 * KX), 2 * KX), :]
    for tile in range(2):
        start = 2 * tile * KX
        even = rows_ref[start : start + KX, :]
        odd = pltpu.roll(rows_ref[start + KX : start + 2 * KX, :], LANES // 2, axis=1)
        lane = lax.broadcasted_iota(jnp.int32, even.shape, 1)
        modes = jnp.where(lane < LANES // 2, even, odd)
        both = jnp.concatenate([modes, crossed(modes, channels, -1.0)], axis=0)
        out_ref[pl.ds(tile, length, stride=2), :] = lax.dot_general(
            basis,
            both,
            (((0,), (0,)), ((), ())),
            precision=highest,
            preferred_element_type=f32,
        )


def middle_kernel(rows_ref, table_ref, weight_ref, out_ref, *, channels, norm_factor):
    share = weight_ref.shape[0]
    half = lax.rem(lax.axis_index("gy"), KX // share)
    basis = table_ref[pl.ds(pl.multiple_of(half * 2 * share, 2 * share), 2 * share), :]
    sums = jnp.dot(basis, rows_ref[...], precision=highest, preferred_element_type=f32)
    sums = norm_factor * (sums[:share] + crossed(sums[share:], channels, 1.0))
    hat_real = sums[:, :channels]
    hat_imag = sums[:, channels : 2 * channels]
    size = channels * channels
    lane = lax.broadcasted_iota(jnp.int32, (channels, size), 1)
    row = lax.broadcasted_iota(jnp.int32, (channels, size), 0)
    spread = jnp.where(lane // channels == row, 1.0, 0.0).astype(f32)
    hat = jnp.dot(
        jnp.concatenate([hat_real, hat_imag], axis=0),
        spread,
        precision=highest,
        preferred_element_type=f32,
    )
    real = hat[:share]
    imag = hat[share:]
    weight_real = weight_ref[:, :size]
    weight_imag = weight_ref[:, size:]
    terms = jnp.concatenate(
        [real * weight_real - imag * weight_imag, real * weight_imag + imag * weight_real], axis=0
    )
    mixed = terms[:, :LANES]
    for start in range(LANES, size, LANES):
        mixed = mixed + terms[:, start : start + LANES]
    step = LANES // 2
    while step >= channels:
        mixed = mixed + pltpu.roll(mixed, step, axis=1)
        step = step // 2
    lane = lax.broadcasted_iota(jnp.int32, (share, LANES), 1)
    mixed_real = mixed[:share]
    mixed_imag = mixed[share:]
    mixed = jnp.where(lane < channels, mixed_real, mixed_imag)
    for start in range(0, out_ref.shape[0], share):
        out_ref[start : start + share, :] = mixed


def extend_kernel(cells_ref, rows_ref, out_ref, *, count_y):
    rows_y = out_ref.shape[0] - 2
    channels = out_ref.shape[1]
    place = lax.axis_index("gy")
    step = rows_ref.shape[0] // count_y
    below = pl.multiple_of(jnp.maximum(place - 1, 0) * step, 8)
    above = pl.multiple_of(jnp.minimum(place + 1, count_y - 1) * step, 8)
    before = rows_ref[pl.ds(below + step - channels, channels), :]
    after = rows_ref[pl.ds(above + step - channels, channels), :]
    out_ref[0] = jnp.where(place > 0, before, jnp.zeros_like(before))
    out_ref[rows_y + 1] = jnp.where(place < count_y - 1, after, jnp.zeros_like(after))
    for row in range(rows_y):
        out_ref[row + 1] = cells_ref[pl.ds(row, channels, stride=rows_y), :]


def doubled_taps(taps):
    high, low = halves_of(taps)
    return jnp.concatenate([high, high, low], axis=1)


def doubled_cells(cells):
    high, low = halves_of(cells)
    return jnp.concatenate([high, low, high], axis=0)


def shifted_sum(parts, depth):
    lane = lax.broadcasted_iota(jnp.int32, parts[1].shape, 1)
    below = jnp.where(lane == 0, 0.0, pltpu.roll(parts[0], 1, axis=1))
    above = jnp.where(lane == depth - 1, 0.0, pltpu.roll(parts[2], depth - 1, axis=1))
    return parts[1] + below + above


def conv_kernel(left_ref, cells_ref, right_ref, taps_ref, bias_ref, out_ref, sums_scratch):
    planes = (left_ref, cells_ref, right_ref)
    channels, depth = bias_ref.shape
    rows_y = cells_ref.shape[0] - 2
    width = 3 * channels
    taps = doubled_taps(taps_ref[...])

    def collect(row):
        parts = []
        for shift in range(3):
            first = shift * channels
            parts.append(
                sums_scratch[row, first : first + channels, :]
                + sums_scratch[row + 1, width + first : width + first + channels, :]
                + sums_scratch[row + 2, 2 * width + first : 2 * width + first + channels, :]
            )
        out_ref[pl.ds(row, channels, stride=rows_y), :] = shifted_sum(parts, depth) + bias_ref[...]

    for row in range(0, rows_y + 2, 2):
        cells = jnp.concatenate(
            [
                jnp.concatenate([plane[row + side] for plane in planes], axis=0)
                for side in range(2)
            ],
            axis=1,
        )
        sums = product(taps, doubled_cells(cells), ((1,), (0,)))
        sums_scratch[row] = sums[:, :depth]
        sums_scratch[row + 1] = sums[:, depth:]
        if row:
            collect(row - 2)
            collect(row - 1)


def inverse_kernel(
    rows_ref, wide_high, wide_low, deep_high, deep_low, conv_ref,
    out_ref, modes_ref, middle_ref
):
    channels = modes_ref.shape[1] // KY
    groups = channels // GROUP
    for mode in range(KY):
        for part in range(2):
            for odd in range(2):
                lane = odd * 2 * channels + part * channels
                row = (part * 2 + odd) * (KZ // 2)
                modes_ref[row : row + KZ // 2, mode * channels : (mode + 1) * channels] = rows_ref[
                    mode * KZ // 2 : (mode + 1) * KZ // 2, lane : lane + channels
                ]
    deep = product_of_halves(
        halves_of(modes_ref[...]), (deep_high[...], deep_low[...]), ((0,), (0,))
    )
    for group in range(groups):
        for part in range(2):
            for mode in range(KY):
                row = (part * KY + mode) * GROUP
                place = mode * channels + group * GROUP
                middle_ref[row : row + GROUP, group * LANES : (group + 1) * LANES] = deep[
                    place : place + GROUP, part * LANES : (part + 1) * LANES
                ]
    wide = (wide_high[...], wide_low[...])
    block = wide_high.shape[0]
    for first in range(0, groups, 2):
        summed = product_of_halves(
            wide,
            halves_of(middle_ref[:, first * LANES : (first + 2) * LANES]),
            ((1,), (0,)),
        )
        for side in range(2):
            start = (first + side) * block
            value = (
                summed[:, side * LANES : (side + 1) * LANES] + conv_ref[start : start + block, :]
            )
            out_ref[start : start + block, :] = (
                0.5 * value * (1.0 + lax.erf(value * math.sqrt(0.5)))
            )


def local(features, conv_weight, conv_bias, spectral_weight):
    channels, rows_x, rows_y, depth = features.shape
    count_x = lax.axis_size("gx")
    count_y = lax.axis_size("gy")
    length_x = rows_x * count_x
    length_y = rows_y * count_y
    norm_factor = 1.0 / math.sqrt(length_x * length_y * depth)
    pairs = KY * KZ
    devices = count_x * count_y
    halves = devices // pairs
    share = KX // halves
    params = pltpu.CompilerParams(vmem_limit_bytes=48 * 1024 * 1024)
    cells = features.reshape(channels * rows_y, depth)

    wide, deep = forward_tables(rows_y, length_y, depth)
    outgoing = pl.pallas_call(
        forward_kernel,
        out_shape=jax.ShapeDtypeStruct(((pairs // 2 // CLASSES + channels) * count_y, LANES), f32),
        in_specs=[pl.BlockSpec(memory_space=pltpu.HBM)] * 5,
        scratch_shapes=[
            pltpu.VMEM(cells.shape, f32),
            pltpu.VMEM(wide.shape, bf16),
            pltpu.VMEM(wide.shape, bf16),
            pltpu.VMEM(deep.shape, bf16),
            pltpu.VMEM(deep.shape, bf16),
            pltpu.VMEM((KY * channels, 2 * depth), f32),
            pltpu.VMEM((pairs // 2, LANES), f32),
            pltpu.SemaphoreType.DMA((6,)),
        ],
        compiler_params=params,
        name="forward",
    )(*[
        pltpu.with_memory_space_constraint(value, pltpu.HBM)
        for value in (cells, *fixed_halves(wide), *fixed_halves(deep))
    ])
    taps = jnp.transpose(conv_weight, (1, 2, 4, 0, 3)).reshape(9 * channels, 3 * channels)
    bias = jnp.broadcast_to(conv_bias[:, None], (channels, depth))

    def small(kernel, name, rows, *operands):
        return pl.pallas_call(
            kernel,
            out_shape=jax.ShapeDtypeStruct((rows, LANES), f32),
            compiler_params=params,
            cost_estimate=COSTLY.get(name),
            name=name,
        )(*operands)

    right = lax.ppermute(features, "gx", [(i + 1, i) for i in range(count_x - 1)])
    half_table, whole_table = long_tables(length_x, count_y, share)
    gathered = lax.all_to_all(outgoing, "gy", 0, 0, tiled=True)
    plane = jax.ShapeDtypeStruct((rows_y + 2, channels, depth), f32)
    own = pl.pallas_call(
        lambda *refs: extend_kernel(*refs, count_y=count_y),
        out_shape=plane,
        compiler_params=params,
        name="extend",
    )(cells, gathered)
    left = lax.ppermute(own, "gx", [(i, i + 1) for i in range(count_x - 1)])
    right = lax.ppermute(own, "gx", [(i + 1, i) for i in range(count_x - 1)])
    local_term = pl.pallas_call(
        conv_kernel,
        out_shape=jax.ShapeDtypeStruct(cells.shape, f32),
        scratch_shapes=[pltpu.VMEM((rows_y + 2, 9 * channels, depth), f32)],
        compiler_params=params,
        name="conv",
    )(left, own, right, taps, bias)
    folded = small(
        lambda *refs: fold_kernel(*refs, channels=channels),
        "fold", count_x, gathered, *turn_tables(count_y, count_x // 2),
    )
    arrived = lax.all_to_all(folded, "gx", 0, 0, tiled=True)
    mixed = small(
        lambda *refs: middle_kernel(*refs, channels=channels, norm_factor=norm_factor),
        "middle", count_y * share, arrived, half_table, spectral_weight,
    )
    shared = lax.all_to_all(mixed, "gy", 0, 0, tiled=True)
    returning = small(
        lambda *refs: spread_kernel(*refs, channels=channels, rows_x=count_x // KY),
        "spread", pairs // 2, shared, whole_table,
    )
    whole = lax.all_to_all(returning, "gx", 0, 0, tiled=True)

    wide, deep = inverse_tables(rows_y, length_y, depth, norm_factor)
    layer_out = pl.pallas_call(
        inverse_kernel,
        out_shape=jax.ShapeDtypeStruct((channels * rows_y, depth), f32),
        scratch_shapes=[
            pltpu.VMEM((2 * KZ, KY * channels), f32),
            pltpu.VMEM((2 * KY * GROUP, channels // GROUP * LANES), f32),
        ],
        compiler_params=params,
        name="inverse",
    )(whole, *fixed_halves(wide), *fixed_halves(deep), local_term)
    return layer_out.reshape(features.shape)


def solution(mesh):
    return jax.shard_map(
        local,
        mesh=mesh,
        in_specs=(P(None, "gx", "gy", None), P(), P(), P(("gx", "gy"), None)),
        out_specs=P(None, "gx", "gy", None),
        check_vma=False,
    )
```

```python
import math

import jax
import jax.numpy as jnp
import numpy as np
from jax import lax
from jax.experimental import pallas as pl
from jax.experimental.pallas import tpu as pltpu
from jax.sharding import PartitionSpec as P

KX = 16
KY = 16
KZ = 16
GROUP = 8
CLASSES = 4
LANES = 128
LONG = pl.CostEstimate(flops=10**10, transcendentals=0, bytes_accessed=1 << 20)
COSTLY = dict.fromkeys((), LONG)

f32 = jnp.float32
bf16 = jnp.bfloat16
highest = lax.Precision.HIGHEST


def halves_of(value):
    high = value.astype(bf16)
    return high, (value - high.astype(f32)).astype(bf16)


def fixed_halves(table):
    table = np.asarray(table, np.float32)
    high = table.astype(bf16)
    return jnp.asarray(high), jnp.asarray((table - high.astype(np.float32)).astype(bf16))


def product(left, right, dims):
    return lax.dot_general(left, right, (dims, ((), ())), preferred_element_type=f32)


def product_of_halves(left, right, dims):
    return (
        product(left[0], right[0], dims)
        + product(left[0], right[1], dims)
        + product(left[1], right[0], dims)
    )


def signed_modes(number):
    series = np.arange(number)
    return np.where(series < number // 2, series, series - number)


def deep_angles(depth, step):
    order = np.concatenate([np.arange(start, KZ, step) for start in range(step)])
    return order, 2.0 * np.pi / depth * np.outer(order, np.arange(depth))


def forward_tables(rows_y, length_y, depth):
    angle = 2.0 * np.pi / length_y * np.outer(signed_modes(KY), np.arange(rows_y))
    same = np.eye(GROUP)
    wide = np.einsum("rby,ij->rbijy", np.stack([np.cos(angle), -np.sin(angle)]), same)
    wide = wide.reshape(2 * KY * GROUP, GROUP * rows_y)
    _, angle = deep_angles(depth, CLASSES)
    deep_cos = np.cos(angle)
    deep_sin = np.sin(angle)
    deep = np.concatenate(
        [
            np.concatenate([deep_cos, deep_sin], axis=1),
            np.concatenate([-deep_sin, deep_cos], axis=1),
        ],
        axis=0,
    )
    return wide, deep


def inverse_tables(rows_y, length_y, depth, norm_factor):
    angle = 2.0 * np.pi / length_y * np.outer(np.arange(rows_y), signed_modes(KY))
    same = np.eye(GROUP)
    wide = np.einsum("ryb,ij->iyrbj", np.stack([np.cos(angle), -np.sin(angle)]), same)
    wide = wide.reshape(GROUP * rows_y, 2 * KY * GROUP)
    order, angle = deep_angles(depth, 2)
    factor = norm_factor * np.where(order == 0, 1.0, 2.0)[:, None]
    deep_cos = factor * np.cos(angle)
    deep_sin = factor * np.sin(angle)
    deep = np.concatenate(
        [
            np.concatenate([deep_cos, deep_sin], axis=1),
            np.concatenate([-deep_sin, deep_cos], axis=1),
        ],
        axis=0,
    )
    return wide, deep


def long_tables(length_x, count_y, share):
    modes = signed_modes(KX)
    angle = 2.0 * np.pi / length_x * np.outer(modes, np.arange(length_x))
    halves = [
        np.concatenate([np.cos(angle[i : i + share]), np.sin(angle[i : i + share])])
        for i in range(0, KX, share)
    ]
    turned = [angle + 2.0 * np.pi / count_y * turn for turn in range(count_y)]
    whole = [np.concatenate([np.cos(each), np.sin(each)]) for each in turned]
    return jnp.asarray(np.concatenate(halves), f32), jnp.asarray(np.concatenate(whole), f32)


def turn_tables(count_y, rows):
    wide = 2 * (np.arange(rows) // (KZ // CLASSES))[:, None] + np.arange(LANES) // (LANES // 2)
    angle = 2.0 * np.pi / count_y * (np.arange(count_y)[:, None, None] * wide % count_y)
    angle = angle.reshape(count_y * rows, LANES)
    return jnp.asarray(np.cos(angle), f32), jnp.asarray(np.sin(angle), f32)


def forward_kernel(
    cells_hbm, wide_high_hbm, wide_low_hbm, deep_high_hbm, deep_low_hbm, out_ref,
    cells_ref, wide_high, wide_low, deep_high, deep_low, middle_ref, pair_ref, sems
):
    half = cells_ref.shape[0] // 2
    chunks = [pl.ds(0, half), pl.ds(half, half)]
    moves = [
        (wide_high_hbm, wide_high),
        (wide_low_hbm, wide_low),
        (cells_hbm.at[chunks[0]], cells_ref.at[chunks[0]]),
        (cells_hbm.at[chunks[1]], cells_ref.at[chunks[1]]),
        (deep_high_hbm, deep_high),
        (deep_low_hbm, deep_low),
    ]
    copies = [pltpu.make_async_copy(*pair, sems.at[i]) for i, pair in enumerate(moves)]
    for copy in copies:
        copy.start()
    for copy in copies[:3]:
        copy.wait()
    channels = middle_ref.shape[0] // KY
    block = wide_high.shape[1]
    groups = channels // GROUP
    wide = (wide_high[...], wide_low[...])
    for first in range(0, groups, 2):
        if first == groups // 2:
            copies[3].wait()
        cells = jnp.concatenate(
            [
                cells_ref[first * block : (first + 1) * block, :],
                cells_ref[(first + 1) * block : (first + 2) * block, :],
            ],
            axis=1,
        )
        summed = product_of_halves(wide, halves_of(cells), ((1,), (0,)))
        for part in range(2):
            for mode in range(KY):
                row = (part * KY + mode) * GROUP
                for side in range(2):
                    place = mode * channels + (first + side) * GROUP
                    middle_ref[place : place + GROUP, part * LANES : (part + 1) * LANES] = (
                        summed[row : row + GROUP, side * LANES : (side + 1) * LANES]
                    )
    copies[4].wait()
    copies[5].wait()
    modes = product_of_halves(
        (deep_high[...], deep_low[...]), halves_of(middle_ref[...]), ((1,), (1,))
    )
    size = KZ // CLASSES
    rows = KY // 2 * size
    for mode in range(KY):
        for part in range(2):
            for kind in range(CLASSES):
                lane = mode % 2 * 2 * channels + part * channels
                row = kind * rows + mode // 2 * size
                source = part * KZ + kind * size
                pair_ref[row : row + size, lane : lane + channels] = modes[
                    source : source + size, mode * channels : (mode + 1) * channels
                ]
    copies_of = out_ref.shape[0] // (CLASSES * rows)
    for kind in range(CLASSES):
        for each in range(copies_of):
            start = (kind * copies_of + each) * rows
            out_ref[start : start + rows, :] = pair_ref[kind * rows : (kind + 1) * rows, :]


def crossed(value, channels, sign):
    lane = lax.broadcasted_iota(jnp.int32, value.shape, 1)
    width = value.shape[1]
    return jnp.where(
        lane % (2 * channels) < channels,
        sign * pltpu.roll(value, width - channels, axis=1),
        -sign * pltpu.roll(value, channels, axis=1),
    )


def fold_kernel(rows_ref, cos_ref, sin_ref, out_ref, *, channels):
    rows = out_ref.shape[0] // 2
    total = jnp.zeros((rows, LANES), f32)
    for start in range(0, rows_ref.shape[0], rows):
        place = slice(start, start + rows)
        value = rows_ref[place, :]
        total = total + value * cos_ref[place, :] + crossed(value, channels, 1.0) * sin_ref[place, :]
    other = pltpu.roll(total, LANES // 2, axis=1)
    size = KZ // CLASSES
    for tile in range(rows // size):
        start = tile * size
        out_ref[2 * start : 2 * start + size, :] = total[start : start + size, :]
        out_ref[2 * start + size : 2 * start + 2 * size, :] = other[start : start + size, :]


def spread_kernel(rows_ref, table_ref, out_ref, *, channels, rows_x):
    length = table_ref.shape[1]
    turns = table_ref.shape[0] // (2 * KX)
    wide_mode = lax.axis_index("gx") // rows_x
    turn = lax.rem(wide_mode * lax.axis_index("gy"), turns)
    basis = table_ref[pl.ds(pl.multiple_of(turn * 2 * KX, 2 * KX), 2 * KX), :]
    for tile in range(2):
        start = 2 * tile * KX
        even = rows_ref[start : start + KX, :]
        odd = pltpu.roll(rows_ref[start + KX : start + 2 * KX, :], LANES // 2, axis=1)
        lane = lax.broadcasted_iota(jnp.int32, even.shape, 1)
        modes = jnp.where(lane < LANES // 2, even, odd)
        both = jnp.concatenate([modes, crossed(modes, channels, -1.0)], axis=0)
        out_ref[pl.ds(tile, length, stride=2), :] = lax.dot_general(
            basis,
            both,
            (((0,), (0,)), ((), ())),
            precision=highest,
            preferred_element_type=f32,
        )


def middle_kernel(rows_ref, table_ref, weight_ref, out_ref, *, channels, norm_factor):
    share = weight_ref.shape[0]
    half = lax.rem(lax.axis_index("gy"), KX // share)
    basis = table_ref[pl.ds(pl.multiple_of(half * 2 * share, 2 * share), 2 * share), :]
    sums = jnp.dot(basis, rows_ref[...], precision=highest, preferred_element_type=f32)
    sums = norm_factor * (sums[:share] + crossed(sums[share:], channels, 1.0))
    hat_real = sums[:, :channels]
    hat_imag = sums[:, channels : 2 * channels]
    size = channels * channels
    lane = lax.broadcasted_iota(jnp.int32, (channels, size), 1)
    row = lax.broadcasted_iota(jnp.int32, (channels, size), 0)
    spread = jnp.where(lane // channels == row, 1.0, 0.0).astype(f32)
    hat = jnp.dot(
        jnp.concatenate([hat_real, hat_imag], axis=0),
        spread,
        precision=highest,
        preferred_element_type=f32,
    )
    real = hat[:share]
    imag = hat[share:]
    weight_real = weight_ref[:, :size]
    weight_imag = weight_ref[:, size:]
    terms = jnp.concatenate(
        [real * weight_real - imag * weight_imag, real * weight_imag + imag * weight_real], axis=0
    )
    mixed = terms[:, :LANES]
    for start in range(LANES, size, LANES):
        mixed = mixed + terms[:, start : start + LANES]
    step = LANES // 2
    while step >= channels:
        mixed = mixed + pltpu.roll(mixed, step, axis=1)
        step = step // 2
    lane = lax.broadcasted_iota(jnp.int32, (share, LANES), 1)
    mixed_real = mixed[:share]
    mixed_imag = mixed[share:]
    mixed = jnp.where(lane < channels, mixed_real, mixed_imag)
    for start in range(0, out_ref.shape[0], share):
        out_ref[start : start + share, :] = mixed


def edges_kernel(left_ref, cells_ref, right_ref, tails_ref, heads_ref, *, rows_y, channels):
    planes = (left_ref, cells_ref, right_ref)
    for plane in range(3):
        rows = pl.ds(plane * channels, channels)
        heads_ref[rows, :] = planes[plane][pl.ds(0, channels, stride=rows_y), :]
        tails_ref[rows, :] = planes[plane][pl.ds(rows_y - 1, channels, stride=rows_y), :]


def doubled_taps(taps):
    high, low = halves_of(taps)
    return jnp.concatenate([high, high, low], axis=1)


def doubled_cells(cells):
    high, low = halves_of(cells)
    return jnp.concatenate([high, low, high], axis=0)


def shifted_sum(parts, depth):
    lane = lax.broadcasted_iota(jnp.int32, parts[1].shape, 1)
    below = jnp.where(lane == 0, 0.0, pltpu.roll(parts[0], 1, axis=1))
    above = jnp.where(lane == depth - 1, 0.0, pltpu.roll(parts[2], depth - 1, axis=1))
    return parts[1] + below + above


def conv_kernel(*refs, planes, rows_y, channels, depth):
    plane_refs = refs[: len(planes)]
    taps_ref, base_ref, out_ref, sums_scratch = refs[len(planes) :]
    width = 3 * channels
    taps = jnp.concatenate(
        [taps_ref[:, plane * channels : (plane + 1) * channels] for plane in planes], axis=1
    )
    taps = doubled_taps(taps)
    sums_scratch[0, :width, :] = jnp.zeros((width, depth), f32)
    sums_scratch[rows_y + 1, 2 * width :, :] = jnp.zeros((width, depth), f32)

    def row_cells(row):
        return jnp.concatenate(
            [plane[pl.ds(row, channels, stride=rows_y), :] for plane in plane_refs], axis=0
        )

    def collect(row):
        parts = []
        for shift in range(3):
            first = shift * channels
            parts.append(
                sums_scratch[row, first : first + channels, :]
                + sums_scratch[row + 1, width + first : width + first + channels, :]
                + sums_scratch[row + 2, 2 * width + first : 2 * width + first + channels, :]
            )
        place = pl.ds(row, channels, stride=rows_y)
        base = base_ref[place, :] if base_ref.shape == out_ref.shape else base_ref[...]
        out_ref[place, :] = shifted_sum(parts, depth) + base

    for step in range(rows_y // 2):
        cells = jnp.concatenate([row_cells(2 * step), row_cells(2 * step + 1)], axis=1)
        sums = product(taps, doubled_cells(cells), ((1,), (0,)))
        sums_scratch[2 * step + 1] = sums[:, :depth]
        sums_scratch[2 * step + 2] = sums[:, depth:]
        if step:
            collect(2 * step - 2)
            collect(2 * step - 1)
    collect(rows_y - 2)
    collect(rows_y - 1)


def inverse_kernel(
    rows_ref, wide_high, wide_low, deep_high, deep_low, conv_ref, before_ref, after_ref, taps_ref,
    out_hbm, modes_ref, middle_ref, conv_scratch, out_ref, sems, *, rows_y
):
    channels = modes_ref.shape[1] // KY
    groups = channels // GROUP
    depth = conv_ref.shape[1]
    width = 3 * channels
    conv_scratch[...] = conv_ref[...]
    taps = jnp.concatenate([taps_ref[:width, :], taps_ref[2 * width :, :]], axis=0)
    cells = jnp.concatenate([before_ref[...], after_ref[...]], axis=1)
    sums = product(doubled_taps(taps), doubled_cells(cells), ((1,), (0,)))
    for row, values in ((0, sums[:width, :depth]), (rows_y - 1, sums[width:, depth:])):
        place = pl.ds(row, channels, stride=rows_y)
        parts = [values[r * channels : (r + 1) * channels] for r in range(3)]
        conv_scratch[place, :] = conv_scratch[place, :] + shifted_sum(parts, depth)
    for mode in range(KY):
        for part in range(2):
            for odd in range(2):
                lane = odd * 2 * channels + part * channels
                row = (part * 2 + odd) * (KZ // 2)
                modes_ref[row : row + KZ // 2, mode * channels : (mode + 1) * channels] = rows_ref[
                    mode * KZ // 2 : (mode + 1) * KZ // 2, lane : lane + channels
                ]
    deep = product_of_halves(
        halves_of(modes_ref[...]), (deep_high[...], deep_low[...]), ((0,), (0,))
    )
    for group in range(groups):
        for part in range(2):
            for mode in range(KY):
                row = (part * KY + mode) * GROUP
                place = mode * channels + group * GROUP
                middle_ref[row : row + GROUP, group * LANES : (group + 1) * LANES] = deep[
                    place : place + GROUP, part * LANES : (part + 1) * LANES
                ]
    wide = (wide_high[...], wide_low[...])
    block = wide_high.shape[0]
    copies = []
    for first in range(0, groups, 2):
        summed = product_of_halves(
            wide,
            halves_of(middle_ref[:, first * LANES : (first + 2) * LANES]),
            ((1,), (0,)),
        )
        for side in range(2):
            start = (first + side) * block
            value = (
                summed[:, side * LANES : (side + 1) * LANES] + conv_scratch[start : start + block, :]
            )
            out_ref[start : start + block, :] = (
                0.5 * value * (1.0 + lax.erf(value * math.sqrt(0.5)))
            )
        rows = pl.ds(first * block, 2 * block)
        copy = pltpu.make_async_copy(out_ref.at[rows], out_hbm.at[rows], sems.at[first // 2])
        copy.start()
        copies.append(copy)
    for copy in copies:
        copy.wait()


def local(features, conv_weight, conv_bias, spectral_weight):
    channels, rows_x, rows_y, depth = features.shape
    count_x = lax.axis_size("gx")
    count_y = lax.axis_size("gy")
    length_x = rows_x * count_x
    length_y = rows_y * count_y
    norm_factor = 1.0 / math.sqrt(length_x * length_y * depth)
    pairs = KY * KZ
    devices = count_x * count_y
    halves = devices // pairs
    share = KX // halves
    params = pltpu.CompilerParams(vmem_limit_bytes=48 * 1024 * 1024)
    cells = features.reshape(channels * rows_y, depth)

    wide, deep = forward_tables(rows_y, length_y, depth)
    outgoing = pl.pallas_call(
        forward_kernel,
        out_shape=jax.ShapeDtypeStruct((pairs // 2 // CLASSES * count_y, LANES), f32),
        in_specs=[pl.BlockSpec(memory_space=pltpu.HBM)] * 5,
        scratch_shapes=[
            pltpu.VMEM(cells.shape, f32),
            pltpu.VMEM(wide.shape, bf16),
            pltpu.VMEM(wide.shape, bf16),
            pltpu.VMEM(deep.shape, bf16),
            pltpu.VMEM(deep.shape, bf16),
            pltpu.VMEM((KY * channels, 2 * depth), f32),
            pltpu.VMEM((pairs // 2, LANES), f32),
            pltpu.SemaphoreType.DMA((6,)),
        ],
        compiler_params=params,
        name="forward",
    )(*[
        pltpu.with_memory_space_constraint(value, pltpu.HBM)
        for value in (cells, *fixed_halves(wide), *fixed_halves(deep))
    ])
    taps = jnp.transpose(conv_weight, (1, 2, 4, 0, 3)).reshape(9 * channels, 3 * channels)
    bias = jnp.broadcast_to(conv_bias[:, None], (channels, depth))

    def conv(name, planes, *operands):
        return pl.pallas_call(
            lambda *refs: conv_kernel(
                *refs, planes=planes, rows_y=rows_y, channels=channels, depth=depth
            ),
            out_shape=jax.ShapeDtypeStruct(cells.shape, f32),
            scratch_shapes=[pltpu.VMEM((rows_y + 2, 9 * channels, depth), f32)],
            compiler_params=params,
            cost_estimate=COSTLY.get(name),
            name=name,
        )(*operands)

    def small(kernel, name, rows, *operands):
        return pl.pallas_call(
            kernel,
            out_shape=jax.ShapeDtypeStruct((rows, LANES), f32),
            compiler_params=params,
            cost_estimate=COSTLY.get(name),
            name=name,
        )(*operands)

    left = lax.ppermute(features, "gx", [(i, i + 1) for i in range(count_x - 1)])
    half_table, whole_table = long_tables(length_x, count_y, share)
    gathered = lax.all_to_all(outgoing, "gy", 0, 0, tiled=True)
    folded = small(
        lambda *refs: fold_kernel(*refs, channels=channels),
        "fold", count_x, gathered, *turn_tables(count_y, count_x // 2),
    )
    arrived = lax.all_to_all(folded, "gx", 0, 0, tiled=True)
    right_cells, arrived = lax.optimization_barrier((features, arrived))
    right = lax.ppermute(right_cells, "gx", [(i + 1, i) for i in range(count_x - 1)])
    mixed = small(
        lambda *refs: middle_kernel(*refs, channels=channels, norm_factor=norm_factor),
        "middle", count_y * share, arrived, half_table, spectral_weight,
    )
    left = left.reshape(cells.shape)
    right = right.reshape(cells.shape)
    edge = jax.ShapeDtypeStruct((3 * channels, depth), f32)
    tails, heads = pl.pallas_call(
        lambda *refs: edges_kernel(*refs, rows_y=rows_y, channels=channels),
        out_shape=(edge, edge),
        compiler_params=params,
        name="edges",
    )(left, cells, right)
    before = lax.ppermute(tails, "gy", [(i, i + 1) for i in range(count_y - 1)])
    after = lax.ppermute(heads, "gy", [(i + 1, i) for i in range(count_y - 1)])
    local_term = conv("conv", (0, 1, 2), left, cells, right, taps, bias)

    shared = lax.all_to_all(mixed, "gy", 0, 0, tiled=True)
    returning = small(
        lambda *refs: spread_kernel(*refs, channels=channels, rows_x=count_x // KY),
        "spread", pairs // 2, shared, whole_table,
    )
    whole = lax.all_to_all(returning, "gx", 0, 0, tiled=True)

    wide, deep = inverse_tables(rows_y, length_y, depth, norm_factor)
    layer_out = pl.pallas_call(
        lambda *refs: inverse_kernel(*refs, rows_y=rows_y),
        out_shape=jax.ShapeDtypeStruct((channels * rows_y, depth), f32),
        scratch_shapes=[
            pltpu.VMEM((2 * KZ, KY * channels), f32),
            pltpu.VMEM((2 * KY * GROUP, channels // GROUP * LANES), f32),
            pltpu.VMEM((channels * rows_y, depth), f32),
            pltpu.VMEM((channels * rows_y, depth), f32),
            pltpu.SemaphoreType.DMA((2,)),
        ],
        out_specs=pl.BlockSpec(memory_space=pltpu.HBM),
        compiler_params=params,
        name="inverse",
    )(whole, *fixed_halves(wide), *fixed_halves(deep), local_term, before, after, taps)
    return layer_out.reshape(features.shape)


def solution(mesh):
    return jax.shard_map(
        local,
        mesh=mesh,
        in_specs=(P(None, "gx", "gy", None), P(), P(), P(("gx", "gy"), None)),
        out_specs=P(None, "gx", "gy", None),
        check_vma=False,
    )
```

```python
import math

import jax
import jax.numpy as jnp
import numpy as np
from jax import lax
from jax.experimental import pallas as pl
from jax.experimental.pallas import tpu as pltpu
from jax.sharding import PartitionSpec as P

KX = 16
KY = 16
KZ = 16
GROUP = 8
CLASSES = 4
LANES = 128
LONG = pl.CostEstimate(flops=10**10, transcendentals=0, bytes_accessed=1 << 20)
COSTLY = dict.fromkeys((), LONG)

f32 = jnp.float32
bf16 = jnp.bfloat16
highest = lax.Precision.HIGHEST


def halves_of(value):
    high = value.astype(bf16)
    return high, (value - high.astype(f32)).astype(bf16)


def fixed_halves(table):
    table = np.asarray(table, np.float32)
    high = table.astype(bf16)
    return jnp.asarray(high), jnp.asarray((table - high.astype(np.float32)).astype(bf16))


def product(left, right, dims):
    return lax.dot_general(left, right, (dims, ((), ())), preferred_element_type=f32)


def product_of_halves(left, right, dims):
    return (
        product(left[0], right[0], dims)
        + product(left[0], right[1], dims)
        + product(left[1], right[0], dims)
    )


def signed_modes(number):
    series = np.arange(number)
    return np.where(series < number // 2, series, series - number)


def deep_angles(depth, step):
    order = np.concatenate([np.arange(start, KZ, step) for start in range(step)])
    return order, 2.0 * np.pi / depth * np.outer(order, np.arange(depth))


def forward_tables(rows_y, length_y, depth):
    angle = 2.0 * np.pi / length_y * np.outer(signed_modes(KY), np.arange(rows_y))
    same = np.eye(GROUP)
    wide = np.einsum("rby,ij->rbijy", np.stack([np.cos(angle), -np.sin(angle)]), same)
    wide = wide.reshape(2 * KY * GROUP, GROUP * rows_y)
    _, angle = deep_angles(depth, CLASSES)
    deep_cos = np.cos(angle)
    deep_sin = np.sin(angle)
    deep = np.concatenate(
        [
            np.concatenate([deep_cos, deep_sin], axis=1),
            np.concatenate([-deep_sin, deep_cos], axis=1),
        ],
        axis=0,
    )
    return wide, deep


def inverse_tables(rows_y, length_y, depth, norm_factor):
    angle = 2.0 * np.pi / length_y * np.outer(np.arange(rows_y), signed_modes(KY))
    same = np.eye(GROUP)
    wide = np.einsum("ryb,ij->iyrbj", np.stack([np.cos(angle), -np.sin(angle)]), same)
    wide = wide.reshape(GROUP * rows_y, 2 * KY * GROUP)
    order, angle = deep_angles(depth, 2)
    factor = norm_factor * np.where(order == 0, 1.0, 2.0)[:, None]
    deep_cos = factor * np.cos(angle)
    deep_sin = factor * np.sin(angle)
    deep = np.concatenate(
        [
            np.concatenate([deep_cos, deep_sin], axis=1),
            np.concatenate([-deep_sin, deep_cos], axis=1),
        ],
        axis=0,
    )
    return wide, deep


def long_tables(length_x, count_y, share):
    modes = signed_modes(KX)
    angle = 2.0 * np.pi / length_x * np.outer(modes, np.arange(length_x))
    halves = [
        np.concatenate([np.cos(angle[i : i + share]), np.sin(angle[i : i + share])])
        for i in range(0, KX, share)
    ]
    turned = [angle + 2.0 * np.pi / count_y * turn for turn in range(count_y)]
    whole = [np.concatenate([np.cos(each), np.sin(each)]) for each in turned]
    return jnp.asarray(np.concatenate(halves), f32), jnp.asarray(np.concatenate(whole), f32)


def turn_tables(count_y, rows):
    wide = 2 * (np.arange(rows) // (KZ // CLASSES))[:, None] + np.arange(LANES) // (LANES // 2)
    angle = 2.0 * np.pi / count_y * (np.arange(count_y)[:, None, None] * wide % count_y)
    angle = angle.reshape(count_y * rows, LANES)
    return jnp.asarray(np.cos(angle), f32), jnp.asarray(np.sin(angle), f32)


def forward_kernel(
    cells_hbm, wide_high_hbm, wide_low_hbm, deep_high_hbm, deep_low_hbm, out_ref,
    cells_ref, wide_high, wide_low, deep_high, deep_low, middle_ref, pair_ref, sems
):
    half = cells_ref.shape[0] // 2
    chunks = [pl.ds(0, half), pl.ds(half, half)]
    moves = [
        (wide_high_hbm, wide_high),
        (wide_low_hbm, wide_low),
        (cells_hbm.at[chunks[0]], cells_ref.at[chunks[0]]),
        (cells_hbm.at[chunks[1]], cells_ref.at[chunks[1]]),
        (deep_high_hbm, deep_high),
        (deep_low_hbm, deep_low),
    ]
    copies = [pltpu.make_async_copy(*pair, sems.at[i]) for i, pair in enumerate(moves)]
    for copy in copies:
        copy.start()
    for copy in copies[:3]:
        copy.wait()
    channels = middle_ref.shape[0] // KY
    block = wide_high.shape[1]
    groups = channels // GROUP
    wide = (wide_high[...], wide_low[...])
    for first in range(0, groups, 2):
        if first == groups // 2:
            copies[3].wait()
        cells = jnp.concatenate(
            [
                cells_ref[first * block : (first + 1) * block, :],
                cells_ref[(first + 1) * block : (first + 2) * block, :],
            ],
            axis=1,
        )
        summed = product_of_halves(wide, halves_of(cells), ((1,), (0,)))
        for part in range(2):
            for mode in range(KY):
                row = (part * KY + mode) * GROUP
                for side in range(2):
                    place = mode * channels + (first + side) * GROUP
                    middle_ref[place : place + GROUP, part * LANES : (part + 1) * LANES] = (
                        summed[row : row + GROUP, side * LANES : (side + 1) * LANES]
                    )
    copies[4].wait()
    copies[5].wait()
    modes = product_of_halves(
        (deep_high[...], deep_low[...]), halves_of(middle_ref[...]), ((1,), (1,))
    )
    size = KZ // CLASSES
    rows = KY // 2 * size
    for mode in range(KY):
        for part in range(2):
            for kind in range(CLASSES):
                lane = mode % 2 * 2 * channels + part * channels
                row = kind * rows + mode // 2 * size
                source = part * KZ + kind * size
                pair_ref[row : row + size, lane : lane + channels] = modes[
                    source : source + size, mode * channels : (mode + 1) * channels
                ]
    copies_of = out_ref.shape[0] // (CLASSES * rows)
    for kind in range(CLASSES):
        for each in range(copies_of):
            start = (kind * copies_of + each) * rows
            out_ref[start : start + rows, :] = pair_ref[kind * rows : (kind + 1) * rows, :]


def crossed(value, channels, sign):
    lane = lax.broadcasted_iota(jnp.int32, value.shape, 1)
    width = value.shape[1]
    return jnp.where(
        lane % (2 * channels) < channels,
        sign * pltpu.roll(value, width - channels, axis=1),
        -sign * pltpu.roll(value, channels, axis=1),
    )


def fold_kernel(rows_ref, cos_ref, sin_ref, out_ref, *, channels):
    rows = out_ref.shape[0] // 2
    total = jnp.zeros((rows, LANES), f32)
    for start in range(0, rows_ref.shape[0], rows):
        place = slice(start, start + rows)
        value = rows_ref[place, :]
        total = total + value * cos_ref[place, :] + crossed(value, channels, 1.0) * sin_ref[place, :]
    other = pltpu.roll(total, LANES // 2, axis=1)
    size = KZ // CLASSES
    for tile in range(rows // size):
        start = tile * size
        out_ref[2 * start : 2 * start + size, :] = total[start : start + size, :]
        out_ref[2 * start + size : 2 * start + 2 * size, :] = other[start : start + size, :]


def spread_kernel(rows_ref, table_ref, out_ref, *, channels, rows_x):
    length = table_ref.shape[1]
    turns = table_ref.shape[0] // (2 * KX)
    wide_mode = lax.axis_index("gx") // rows_x
    turn = lax.rem(wide_mode * lax.axis_index("gy"), turns)
    basis = table_ref[pl.ds(pl.multiple_of(turn * 2 * KX, 2 * KX), 2 * KX), :]
    for tile in range(2):
        start = 2 * tile * KX
        even = rows_ref[start : start + KX, :]
        odd = pltpu.roll(rows_ref[start + KX : start + 2 * KX, :], LANES // 2, axis=1)
        lane = lax.broadcasted_iota(jnp.int32, even.shape, 1)
        modes = jnp.where(lane < LANES // 2, even, odd)
        both = jnp.concatenate([modes, crossed(modes, channels, -1.0)], axis=0)
        out_ref[pl.ds(tile, length, stride=2), :] = product_of_halves(
            halves_of(basis), halves_of(both), ((0,), (0,))
        )


def middle_kernel(rows_ref, table_ref, weight_ref, out_ref, *, channels, norm_factor):
    share = weight_ref.shape[0]
    half = lax.rem(lax.axis_index("gy"), KX // share)
    basis = table_ref[pl.ds(pl.multiple_of(half * 2 * share, 2 * share), 2 * share), :]
    sums = product_of_halves(halves_of(basis), halves_of(rows_ref[...]), ((1,), (0,)))
    sums = norm_factor * (sums[:share] + crossed(sums[share:], channels, 1.0))
    hat_real = sums[:, :channels]
    hat_imag = sums[:, channels : 2 * channels]
    size = channels * channels
    lane = lax.broadcasted_iota(jnp.int32, (channels, size), 1)
    row = lax.broadcasted_iota(jnp.int32, (channels, size), 0)
    spread = jnp.where(lane // channels == row, 1.0, 0.0).astype(f32)
    hat = jnp.dot(
        jnp.concatenate([hat_real, hat_imag], axis=0),
        spread,
        precision=highest,
        preferred_element_type=f32,
    )
    real = hat[:share]
    imag = hat[share:]
    weight_real = weight_ref[:, :size]
    weight_imag = weight_ref[:, size:]
    terms = jnp.concatenate(
        [real * weight_real - imag * weight_imag, real * weight_imag + imag * weight_real], axis=0
    )
    mixed = terms[:, :LANES]
    for start in range(LANES, size, LANES):
        mixed = mixed + terms[:, start : start + LANES]
    step = LANES // 2
    while step >= channels:
        mixed = mixed + pltpu.roll(mixed, step, axis=1)
        step = step // 2
    lane = lax.broadcasted_iota(jnp.int32, (share, LANES), 1)
    mixed_real = mixed[:share]
    mixed_imag = mixed[share:]
    mixed = jnp.where(lane < channels, mixed_real, mixed_imag)
    for start in range(0, out_ref.shape[0], share):
        out_ref[start : start + share, :] = mixed


def edges_kernel(left_ref, cells_ref, right_ref, tails_ref, heads_ref, *, rows_y, channels):
    planes = (left_ref, cells_ref, right_ref)
    for plane in range(3):
        rows = pl.ds(plane * channels, channels)
        heads_ref[rows, :] = planes[plane][pl.ds(0, channels, stride=rows_y), :]
        tails_ref[rows, :] = planes[plane][pl.ds(rows_y - 1, channels, stride=rows_y), :]


def doubled_taps(taps):
    high, low = halves_of(taps)
    return jnp.concatenate([high, high, low], axis=1)


def doubled_cells(cells):
    high, low = halves_of(cells)
    return jnp.concatenate([high, low, high], axis=0)


def shifted_sum(parts, depth):
    lane = lax.broadcasted_iota(jnp.int32, parts[1].shape, 1)
    below = jnp.where(lane == 0, 0.0, pltpu.roll(parts[0], 1, axis=1))
    above = jnp.where(lane == depth - 1, 0.0, pltpu.roll(parts[2], depth - 1, axis=1))
    return parts[1] + below + above


def conv_kernel(*refs, planes, rows_y, channels, depth):
    plane_refs = refs[: len(planes)]
    taps_ref, base_ref, out_ref, sums_scratch = refs[len(planes) :]
    width = 3 * channels
    taps = jnp.concatenate(
        [taps_ref[:, plane * channels : (plane + 1) * channels] for plane in planes], axis=1
    )
    taps = doubled_taps(taps)
    sums_scratch[0, :width, :] = jnp.zeros((width, depth), f32)
    sums_scratch[rows_y + 1, 2 * width :, :] = jnp.zeros((width, depth), f32)

    def row_cells(row):
        return jnp.concatenate(
            [plane[pl.ds(row, channels, stride=rows_y), :] for plane in plane_refs], axis=0
        )

    def collect(row):
        parts = []
        for shift in range(3):
            first = shift * channels
            parts.append(
                sums_scratch[row, first : first + channels, :]
                + sums_scratch[row + 1, width + first : width + first + channels, :]
                + sums_scratch[row + 2, 2 * width + first : 2 * width + first + channels, :]
            )
        place = pl.ds(row, channels, stride=rows_y)
        base = base_ref[place, :] if base_ref.shape == out_ref.shape else base_ref[...]
        out_ref[place, :] = shifted_sum(parts, depth) + base

    for step in range(rows_y // 2):
        cells = jnp.concatenate([row_cells(2 * step), row_cells(2 * step + 1)], axis=1)
        sums = product(taps, doubled_cells(cells), ((1,), (0,)))
        sums_scratch[2 * step + 1] = sums[:, :depth]
        sums_scratch[2 * step + 2] = sums[:, depth:]
        if step:
            collect(2 * step - 2)
            collect(2 * step - 1)
    collect(rows_y - 2)
    collect(rows_y - 1)


def inverse_kernel(
    rows_ref, wide_high, wide_low, deep_high, deep_low, conv_ref, before_ref, after_ref, taps_ref,
    out_hbm, modes_ref, middle_ref, conv_scratch, out_ref, sems, *, rows_y
):
    channels = modes_ref.shape[1] // KY
    groups = channels // GROUP
    depth = conv_ref.shape[1]
    width = 3 * channels
    conv_scratch[...] = conv_ref[...]
    taps = jnp.concatenate([taps_ref[:width, :], taps_ref[2 * width :, :]], axis=0)
    cells = jnp.concatenate([before_ref[...], after_ref[...]], axis=1)
    sums = product(doubled_taps(taps), doubled_cells(cells), ((1,), (0,)))
    for row, values in ((0, sums[:width, :depth]), (rows_y - 1, sums[width:, depth:])):
        place = pl.ds(row, channels, stride=rows_y)
        parts = [values[r * channels : (r + 1) * channels] for r in range(3)]
        conv_scratch[place, :] = conv_scratch[place, :] + shifted_sum(parts, depth)
    for mode in range(KY):
        for part in range(2):
            for odd in range(2):
                lane = odd * 2 * channels + part * channels
                row = (part * 2 + odd) * (KZ // 2)
                modes_ref[row : row + KZ // 2, mode * channels : (mode + 1) * channels] = rows_ref[
                    mode * KZ // 2 : (mode + 1) * KZ // 2, lane : lane + channels
                ]
    deep = product_of_halves(
        halves_of(modes_ref[...]), (deep_high[...], deep_low[...]), ((0,), (0,))
    )
    for group in range(groups):
        for part in range(2):
            for mode in range(KY):
                row = (part * KY + mode) * GROUP
                place = mode * channels + group * GROUP
                middle_ref[row : row + GROUP, group * LANES : (group + 1) * LANES] = deep[
                    place : place + GROUP, part * LANES : (part + 1) * LANES
                ]
    wide = (wide_high[...], wide_low[...])
    block = wide_high.shape[0]
    copies = []
    for first in range(0, groups, 2):
        summed = product_of_halves(
            wide,
            halves_of(middle_ref[:, first * LANES : (first + 2) * LANES]),
            ((1,), (0,)),
        )
        for side in range(2):
            start = (first + side) * block
            value = (
                summed[:, side * LANES : (side + 1) * LANES] + conv_scratch[start : start + block, :]
            )
            out_ref[start : start + block, :] = (
                0.5 * value * (1.0 + lax.erf(value * math.sqrt(0.5)))
            )
        rows = pl.ds(first * block, 2 * block)
        copy = pltpu.make_async_copy(out_ref.at[rows], out_hbm.at[rows], sems.at[first // 2])
        copy.start()
        copies.append(copy)
    for copy in copies:
        copy.wait()


def local(features, conv_weight, conv_bias, spectral_weight):
    channels, rows_x, rows_y, depth = features.shape
    count_x = lax.axis_size("gx")
    count_y = lax.axis_size("gy")
    length_x = rows_x * count_x
    length_y = rows_y * count_y
    norm_factor = 1.0 / math.sqrt(length_x * length_y * depth)
    pairs = KY * KZ
    devices = count_x * count_y
    halves = devices // pairs
    share = KX // halves
    params = pltpu.CompilerParams(vmem_limit_bytes=48 * 1024 * 1024)
    cells = features.reshape(channels * rows_y, depth)

    wide, deep = forward_tables(rows_y, length_y, depth)
    outgoing = pl.pallas_call(
        forward_kernel,
        out_shape=jax.ShapeDtypeStruct((pairs // 2 // CLASSES * count_y, LANES), f32),
        in_specs=[pl.BlockSpec(memory_space=pltpu.HBM)] * 5,
        scratch_shapes=[
            pltpu.VMEM(cells.shape, f32),
            pltpu.VMEM(wide.shape, bf16),
            pltpu.VMEM(wide.shape, bf16),
            pltpu.VMEM(deep.shape, bf16),
            pltpu.VMEM(deep.shape, bf16),
            pltpu.VMEM((KY * channels, 2 * depth), f32),
            pltpu.VMEM((pairs // 2, LANES), f32),
            pltpu.SemaphoreType.DMA((6,)),
        ],
        compiler_params=params,
        name="forward",
    )(*[
        pltpu.with_memory_space_constraint(value, pltpu.HBM)
        for value in (cells, *fixed_halves(wide), *fixed_halves(deep))
    ])
    taps = jnp.transpose(conv_weight, (1, 2, 4, 0, 3)).reshape(9 * channels, 3 * channels)
    bias = jnp.broadcast_to(conv_bias[:, None], (channels, depth))

    def conv(name, planes, *operands):
        return pl.pallas_call(
            lambda *refs: conv_kernel(
                *refs, planes=planes, rows_y=rows_y, channels=channels, depth=depth
            ),
            out_shape=jax.ShapeDtypeStruct(cells.shape, f32),
            scratch_shapes=[pltpu.VMEM((rows_y + 2, 9 * channels, depth), f32)],
            compiler_params=params,
            cost_estimate=COSTLY.get(name),
            name=name,
        )(*operands)

    def small(kernel, name, rows, *operands):
        return pl.pallas_call(
            kernel,
            out_shape=jax.ShapeDtypeStruct((rows, LANES), f32),
            compiler_params=params,
            cost_estimate=COSTLY.get(name),
            name=name,
        )(*operands)

    left = lax.ppermute(features, "gx", [(i, i + 1) for i in range(count_x - 1)])
    half_table, whole_table = long_tables(length_x, count_y, share)
    gathered = lax.all_to_all(outgoing, "gy", 0, 0, tiled=True)
    folded = small(
        lambda *refs: fold_kernel(*refs, channels=channels),
        "fold", count_x, gathered, *turn_tables(count_y, count_x // 2),
    )
    arrived = lax.all_to_all(folded, "gx", 0, 0, tiled=True)
    right_cells, arrived = lax.optimization_barrier((features, arrived))
    right = lax.ppermute(right_cells, "gx", [(i + 1, i) for i in range(count_x - 1)])
    mixed = small(
        lambda *refs: middle_kernel(*refs, channels=channels, norm_factor=norm_factor),
        "middle", count_y * share, arrived, half_table, spectral_weight,
    )
    left = left.reshape(cells.shape)
    right = right.reshape(cells.shape)
    edge = jax.ShapeDtypeStruct((3 * channels, depth), f32)
    tails, heads = pl.pallas_call(
        lambda *refs: edges_kernel(*refs, rows_y=rows_y, channels=channels),
        out_shape=(edge, edge),
        compiler_params=params,
        name="edges",
    )(left, cells, right)
    before = lax.ppermute(tails, "gy", [(i, i + 1) for i in range(count_y - 1)])
    after = lax.ppermute(heads, "gy", [(i + 1, i) for i in range(count_y - 1)])
    local_term = conv("conv", (0, 1, 2), left, cells, right, taps, bias)

    shared = lax.all_to_all(mixed, "gy", 0, 0, tiled=True)
    returning = small(
        lambda *refs: spread_kernel(*refs, channels=channels, rows_x=count_x // KY),
        "spread", pairs // 2, shared, whole_table,
    )
    whole = lax.all_to_all(returning, "gx", 0, 0, tiled=True)

    wide, deep = inverse_tables(rows_y, length_y, depth, norm_factor)
    layer_out = pl.pallas_call(
        lambda *refs: inverse_kernel(*refs, rows_y=rows_y),
        out_shape=jax.ShapeDtypeStruct((channels * rows_y, depth), f32),
        scratch_shapes=[
            pltpu.VMEM((2 * KZ, KY * channels), f32),
            pltpu.VMEM((2 * KY * GROUP, channels // GROUP * LANES), f32),
            pltpu.VMEM((channels * rows_y, depth), f32),
            pltpu.VMEM((channels * rows_y, depth), f32),
            pltpu.SemaphoreType.DMA((2,)),
        ],
        out_specs=pl.BlockSpec(memory_space=pltpu.HBM),
        compiler_params=params,
        name="inverse",
    )(whole, *fixed_halves(wide), *fixed_halves(deep), local_term, before, after, taps)
    return layer_out.reshape(features.shape)


def solution(mesh):
    return jax.shard_map(
        local,
        mesh=mesh,
        in_specs=(P(None, "gx", "gy", None), P(), P(), P(("gx", "gy"), None)),
        out_specs=P(None, "gx", "gy", None),
        check_vma=False,
    )
```
